512 devices in a mesh: gx: 32 (over y_hi, z, core), gy: 16 (over y_lo, x).
Axes of the slice: x: 4, y: 8 (y_hi: 2, y_lo: 4; y = y_hi * 4 + y_lo), z: 8, core: 2. Of those that a mesh axis runs over, the one named last changes fastest.
Arguments:
- feature: bfloat16 [6, 64, 768, 2048], P(None, None, 'gx', 'gy'), may hold values from -6 to 6
- widths: int32 [32], replicated, may hold values from 8 to 24, as said below
- dw_weight: float32 [27, 64], replicated, may hold values from -1.25 to 1.25
- dw_bias: float32 [64], replicated, may hold values from -3 to 3
- pw_weight: bfloat16 [64, 64], replicated, may hold values from -0.75 to 0.75
- pw_bias: float32 [64], replicated, may hold values from -3 to 3
- lift_weight: float32 [64, 3], replicated, may hold values from -3 to 3
- coarse: float32 [3, 32, 128], P(None, 'gy'), may hold values from -6 to 6
Outputs:
- block_out: bfloat16 [2, 64, 768, 2048], P(None, None, 'gx', 'gy')
The draws below stay inside these ranges and needn't reach their ends.
Inputs may be any that keep to these rules, and one draw needn't show every extreme that they name: The widths sum to 512; some slab has width exactly 24 and some exactly 8.
All inputs are finite; a program needn't handle non-finite values.
Results may differ from the reference program's by a relative error of at most 0.0031.
Values may be sent and summed in bfloat16 or wider, within the bound.
A program may use at most 64 MiB of HBM per device.

```python
import jax
import jax.numpy as jnp
from jax import lax

C = 64
XW = 16
ZOUT = 2
CF = 16
ZIN = 6
XMAX = 24
NY = 2048
NCX = 32
NCY = 128
N_GX = 32


def draw_widths(key, part):
    first = jax.random.fold_in(key, 11)
    second = jax.random.fold_in(key, 23)
    spread = jax.random.randint(first, (N_GX // 2,), 0, XMAX - XW + 1).astype(jnp.int32)
    spread = spread.at[0].set(XMAX - XW)
    paired = jnp.stack([XW + spread, XW - spread], axis=1).reshape(N_GX)
    order = jax.random.permutation(second, N_GX)
    return paired[order].astype(jnp.int32)


def levels(own_key, extent, cuts, low, top_value):
    level = 1.0
    for position, shards_of in cuts:
        heights = jax.random.uniform(jax.random.fold_in(jax.random.fold_in(own_key, 6), position), (shards_of,), jnp.float32, low / len(cuts), top_value / len(cuts))
        level = level * jnp.repeat(jnp.exp(heights), extent[position] // shards_of).reshape((-1,) + (1,) * (len(extent) - 1 - position))
    return level


def bell_draw(own_key, dims, scale, most, shards=(), held_as=jnp.bfloat16):
    gain = levels(own_key, dims, shards, -0.22, 0.18) if shards else 1.0
    result = jax.random.normal(own_key, dims, jnp.float32) * scale * gain
    return jnp.minimum(jnp.maximum(result, -most), most).astype(held_as)


def setup_inputs(seed: int = 0) -> dict:
    splits = jax.random.split(jax.random.key(seed), 9)
    feature = bell_draw(splits[0], (ZIN, C, N_GX * XMAX, NY), 1.0, 6.0, ((2, 32), (3, 16)))
    widths = draw_widths(jax.random.fold_in(splits[8], 71), 0)
    dw_weight = bell_draw(splits[2], (27, C), 27 ** -0.5, 1.25, (), jnp.float32)
    dw_bias = bell_draw(splits[3], (C,), 0.5, 3.0, (), jnp.float32)
    pw_weight = bell_draw(splits[4], (C, C), C ** -0.5, 0.75)
    pw_bias = bell_draw(splits[5], (C,), 0.5, 3.0, (), jnp.float32)
    lift_weight = bell_draw(splits[6], (C, 3), 0.5, 3.0, (), jnp.float32)
    coarse = bell_draw(splits[7], (3, NCX, NCY), 1.0, 6.0, ((1, 16),), jnp.float32)
    return dict(feature=feature, widths=widths, dw_weight=dw_weight, dw_bias=dw_bias, pw_weight=pw_weight, pw_bias=pw_bias, lift_weight=lift_weight, coarse=coarse)


def reference(feature, widths, dw_weight, dw_bias, pw_weight, pw_bias, lift_weight, coarse):
    total = XW * N_GX
    starts = (jnp.cumsum(widths) - widths).astype(jnp.int32)
    places = jnp.arange(total, dtype=jnp.int32)
    owner = (jnp.sum((starts[None, :] <= places[:, None]).astype(jnp.int32), axis=1) - 1).astype(jnp.int32)
    source = (owner * XMAX + places - starts[owner]).astype(jnp.int32)
    field = jnp.take(feature, source, axis=2)
    depth = jnp.zeros((ZOUT, C, total, NY), jnp.float32) + dw_bias[None, :, None, None]
    for dz in (-1, 0, 1):
        plane = field[2 + 2 * dz:2 + 2 * dz + ZOUT].astype(jnp.float32)
        for dx in (-1, 0, 1):
            for dy in (-1, 0, 1):
                tap = 9 * (dz + 1) + 3 * (dx + 1) + (dy + 1)
                moved = jnp.roll(plane, (-2 * dx, -2 * dy), axis=(2, 3))
                depth = depth + dw_weight[tap][None, :, None, None] * moved
    depth = depth.astype(jnp.bfloat16)
    mixed = jnp.einsum("oc,zcxy->zoxy", pw_weight.astype(jnp.float32), depth.astype(jnp.float32))
    mixed = mixed + pw_bias[None, :, None, None]
    active = jnp.where(mixed > 0, mixed, 0.2 * mixed)
    xcells = jnp.arange(total, dtype=jnp.int32) // CF
    ycells = jnp.arange(NY, dtype=jnp.int32) // CF
    upsampled = jnp.take(jnp.take(coarse, xcells, axis=1), ycells, axis=2)
    lifted = jnp.einsum("ck,kxy->cxy", lift_weight, upsampled, precision=lax.Precision.HIGHEST)
    value = field[2:2 + ZOUT].astype(jnp.float32) + active + lifted[None]
    slots = jnp.arange(N_GX * XMAX, dtype=jnp.int32)
    slab = slots // XMAX
    inner = slots % XMAX
    valid = inner < widths[slab]
    target = jnp.clip(starts[slab] + inner, 0, total - 1).astype(jnp.int32)
    placed = jnp.take(value, target, axis=2)
    return jnp.where(valid[None, None, :, None], placed, 0.0).astype(jnp.bfloat16)
```

```python
import functools

import jax
import jax.numpy as jnp
from jax import lax
from jax.experimental import pallas as pl
from jax.experimental.pallas import tpu as pltpu
from jax.sharding import PartitionSpec as P

MESH = pl.DeviceIdType.MESH
XW = 16
ZIN = 6
ZOUT = 2
C = 64
CF = 16
SUB = 8
F32 = jnp.float32
BF16 = jnp.bfloat16
HIGH = lax.Precision.HIGHEST
NN = (((1,), (0,)), ((), ()))
NT = (((1,), (1,)), ((), ()))
TN = (((0,), (0,)), ((), ()))


def iota(shape, dim):
    return lax.broadcasted_iota(jnp.int32, shape, dim)


def dot(a, b, dims=NN, precision=None):
    return lax.dot_general(a, b, dims, precision=precision, preferred_element_type=F32)


def tap(dz, dx, dy):
    return 9 * (dz + 1) + 3 * (dx + 1) + (dy + 1)


def depth_kernel(
    nx, ny,
    widths, dw_s, bias_s, dw_v, coarse, feat,
    depth_ref, up_ref,
    field, local, rim, wide, place, stage, rim_edge, edge,
    row_send, row_recv, corn_send, corn_recv, col_send, col_recv, own, coarse_all,
    field_sem, row_ssem, row_rsem, corn_ssem, corn_rsem, col_ssem, col_rsem, co_ssem, co_rsem,
):
    lanes = feat.shape[3]
    blocks = feat.shape[2] // SUB
    block = C * SUB
    gx, gy = lax.axis_index("gx"), lax.axis_index("gy")
    above = lax.rem(gx + 1, nx)
    below = lax.rem(gx + nx - 1, nx)
    sides = (below, above)

    def along(k):
        return lax.rem(gy + k, ny)

    lefts = (along(ny - 1), along(1))

    barrier = pltpu.get_barrier_semaphore()
    for k in range(1, ny):
        pl.semaphore_signal(barrier, inc=1, device_id=(gx, along(k)), device_id_type=MESH)
    for x in sides:
        for y in (gy,) + lefts:
            pl.semaphore_signal(barrier, inc=1, device_id=(x, y), device_id_type=MESH)

    loads = []
    for p in range(ZIN):
        for b in range(blocks):
            loads.append(
                pltpu.make_async_copy(
                    feat.at[p, :, pl.ds(SUB * b, SUB), :], field.at[p, b], field_sem.at[p, b]
                )
            )
            loads[-1].start()

    width = widths[gx]
    start = jnp.int32(0)
    for d in range(nx):
        start = start + jnp.where(d < gx, widths[d], 0)

    rows = coarse.shape[1]
    own[...] = jnp.zeros_like(own)
    for k in range(3):
        own[pl.ds(k * rows, rows), :] = coarse[k]

    eye = (iota((C, C), 0) == iota((C, C), 1)).astype(F32)
    by_channel = dot(eye, dw_v[...], NT, HIGH)
    for side, dx in ((0, 1), (1, -1)):
        for dz in (-1, 0, 1):
            for dy in (-1, 0, 1):
                t = tap(dz, dx, dy)
                wide[side, 3 * (dz + 1) + dy + 1] = jnp.broadcast_to(
                    by_channel[:, t : t + 1], (C, lanes)
                )
    spread = (iota((C, block), 0) == iota((C, block), 1) // SUB).astype(F32)
    by_lane = dot(dw_v[...], spread, NN, HIGH)

    half = C // 2
    pick_row = iota((2 * half, half * SUB), 0)
    pick_col = iota((2 * half, half * SUB), 1)
    same = (pick_row % half) == (pick_col // SUB)

    def picks(first, b):
        hit = same & ((pick_col % SUB) + SUB * b == first + pick_row // half)
        return jnp.where(hit, 1.0, 0.0).astype(BF16)

    pick_top = picks(0, 0)
    pick_bottom = [picks(width - 2, b) for b in range(blocks)]

    for at in range(ZIN * blocks):
        loads[at].wait()

    for p in range(ZIN):
        for h in range(2):
            part = [
                field[p, b, pl.ds(h * half, half)].reshape(half * SUB, lanes) for b in range(blocks)
            ]
            top = dot(pick_top, part[0])
            bottom = dot(pick_bottom[0], part[0])
            for b in range(1, blocks):
                bottom = bottom + dot(pick_bottom[b], part[b])
            for r in range(2):
                rim[0, p, r, pl.ds(h * half, half), :] = top[r * half : (r + 1) * half]
                rim[1, p, r, pl.ds(h * half, half), :] = bottom[r * half : (r + 1) * half]

    lane = iota((C, lanes), 1)
    for side in range(2):
        for z in range(ZOUT):
            for r in range(2):
                sums = [None, None, None]
                for dz in (-1, 0, 1):
                    cells = rim[side, z + 2 + 2 * dz, r]
                    for dy in (-1, 0, 1):
                        term = wide[side, 3 * (dz + 1) + dy + 1] * cells
                        sums[dy + 1] = term if sums[dy + 1] is None else sums[dy + 1] + term
                at = pl.ds(z * 2 * C + r * C, C)
                total = sums[1]
                total = total + jnp.where(lane < lanes - 2, pltpu.roll(sums[2], lanes - 2, 1), 0.0)
                total = total + jnp.where(lane >= 2, pltpu.roll(sums[0], 2, 1), 0.0)
                row_send[side, at, :] = total.astype(BF16)
                rim_edge[side, 0, at, :] = sums[2].astype(BF16)
                rim_edge[side, 1, at, :] = sums[0].astype(BF16)

    pl.semaphore_wait(barrier, ny - 1 + 6)

    copies = []
    for k in range(1, ny):
        copies.append(
            pltpu.make_async_remote_copy(
                src_ref=own, dst_ref=coarse_all.at[gy], send_sem=co_ssem.at[k - 1],
                recv_sem=co_rsem.at[k - 1], device_id=(gx, along(k)), device_id_type=MESH,
            )
        )
        copies[-1].start()
    coarse_all[gy] = own[...]
    for side in range(2):
        copies.append(
            pltpu.make_async_remote_copy(
                src_ref=row_send.at[side], dst_ref=row_recv.at[1 - side],
                send_sem=row_ssem.at[side], recv_sem=row_rsem.at[1 - side],
                device_id=(sides[side], gy), device_id_type=MESH,
            )
        )
        copies[-1].start()

    ends_row, ends_lane = iota((16, lanes), 0), iota((16, lanes), 1)
    ends = [
        jnp.where((ends_row < 2) & (ends_lane == ends_row + first), 1.0, 0.0).astype(BF16)
        for first in (0, lanes - 2)
    ]
    for side in range(2):
        for e in range(2):
            corn_send[side, e] = dot(ends[e], rim_edge[side, e], NT)[:SUB]
    for side in range(2):
        for e in range(2):
            copies.append(
                pltpu.make_async_remote_copy(
                    src_ref=corn_send.at[side, e], dst_ref=corn_recv.at[1 - side, 1 - e],
                    send_sem=corn_ssem.at[side, e], recv_sem=corn_rsem.at[1 - side, 1 - e],
                    device_id=(sides[side], lefts[e]), device_id_type=MESH,
                )
            )
            copies[-1].start()

    both = jnp.where(
        ((ends_row < 2) & (ends_lane == ends_row))
        | ((ends_row >= 2) & (ends_row < 4) & (ends_lane == ends_row + lanes - 4)),
        1.0, 0.0,
    ).astype(BF16)
    in_block = iota((SUB, block), 1) % SUB
    for p in range(ZIN):
        for b in range(blocks):
            found = dot(both, field[p, b].reshape(block, lanes), NT)[:SUB]
            edge[p, b] = jnp.where(in_block + SUB * b < width, found, 0.0)
    first_two = iota((SUB, block), 0) < 2
    weight = {}
    for dz in (-1, 0, 1):
        for dx in (-1, 0, 1):
            high, low = tap(dz, dx, 1), tap(dz, dx, -1)
            weight[dz, dx] = jnp.where(
                first_two,
                jnp.broadcast_to(by_lane[high : high + 1], (SUB, block)),
                jnp.broadcast_to(by_lane[low : low + 1], (SUB, block)),
            )
    for z in range(ZOUT):
        sums = {}
        for dx in (-1, 0, 1):
            for b in range(blocks):
                total = weight[-1, dx] * edge[z, b]
                total = total + weight[0, dx] * edge[z + 2, b]
                sums[dx, b] = total + weight[1, dx] * edge[z + 4, b]
        for b in range(blocks):
            total = sums[0, b]
            total = total + jnp.where(in_block < 6, pltpu.roll(sums[1, b], block - 2, 1), 0.0)
            total = total + jnp.where(in_block >= 2, pltpu.roll(sums[-1, b], 2, 1), 0.0)
            if b + 1 < blocks:
                total = total + jnp.where(in_block >= 6, pltpu.roll(sums[1, b + 1], 6, 1), 0.0)
            if b > 0:
                total = total + jnp.where(
                    in_block < 2, pltpu.roll(sums[-1, b - 1], block - 6, 1), 0.0
                )
            at = pl.ds((z * blocks + b) * block, block)
            col_send[0, :, at] = total[0:2]
            col_send[1, :, at] = total[2:4]
    for e in range(2):
        copies.append(
            pltpu.make_async_remote_copy(
                src_ref=col_send.at[e], dst_ref=col_recv.at[1 - e],
                send_sem=col_ssem.at[e], recv_sem=col_rsem.at[1 - e],
                device_id=(gx, lefts[e]), device_id_type=MESH,
            )
        )
        copies[-1].start()

    stage[...] = jnp.zeros_like(stage)
    slot = iota((2, SUB, lanes), 1)
    line = iota((blocks * SUB, lanes), 1)

    def pair(i, carry):
        c0 = 2 * i
        for p in range(ZIN):
            for b in range(blocks):
                cells = field[p, b, pl.ds(c0, 2)].astype(F32)
                if b > 0:
                    cells = jnp.where(slot + SUB * b < width, cells, 0.0)
                for h in range(2):
                    stage[h, p, pl.ds(SUB * (b + 1), SUB), :] = cells[h]
        for h in range(2):
            for z in range(ZOUT):
                sums = [None, None, None]
                for dz in (-1, 0, 1):
                    for dx in (-1, 0, 1):
                        cells = stage[h, z + 2 + 2 * dz, pl.ds(SUB + 2 * dx, SUB * blocks), :]
                        for dy in (-1, 0, 1):
                            term = dw_s[tap(dz, dx, dy), c0 + h] * cells
                            sums[dy + 1] = term if sums[dy + 1] is None else sums[dy + 1] + term
                total = sums[1] + bias_s[c0 + h]
                total = total + jnp.where(line < lanes - 2, pltpu.roll(sums[2], lanes - 2, 1), 0.0)
                total = total + jnp.where(line >= 2, pltpu.roll(sums[0], 2, 1), 0.0)
                for b in range(blocks):
                    local[z, b, c0 + h] = total[SUB * b : SUB * (b + 1)]
        return carry

    lax.fori_loop(0, C // 2, pair, 0)

    put_row, put_col = iota((block, 4 * C), 0), iota((block, 4 * C), 1)
    alike = (put_row // SUB) == (put_col % C)
    target = jnp.where(put_col < 2 * C, put_col // C, width - 2 + (put_col // C) - 2)
    for b in range(blocks):
        hit = alike & ((put_row % SUB) + SUB * b == target)
        place[b] = jnp.where(hit, 1.0, 0.0).astype(BF16)

    for copy in copies:
        copy.wait_recv()

    ncols = coarse_all.shape[2]
    held = coarse_all[...].reshape(ny * SUB, ncols)
    column = (
        iota((ncols, lanes), 0) == gy * (lanes // CF) + iota((ncols, lanes), 1) // CF
    ).astype(F32)
    count = blocks * SUB
    up_row, up_col = iota((3 * count, ny * SUB), 0), iota((3 * count, ny * SUB), 1)
    cell = start + up_row % count
    cell = jnp.where(cell >= XW * nx, cell - XW * nx, cell) // CF
    hit = (up_col // SUB == cell // rows) & (up_col % SUB == (up_row // count) * rows + cell % rows)
    along_y = dot(held, column, NN, HIGH)
    up_ref[...] = dot(jnp.where(hit, 1.0, 0.0), along_y, NN, HIGH)

    back = [
        jnp.where((iota((SUB, lanes), 0) < 2) & (iota((SUB, lanes), 1) == iota((SUB, lanes), 0) + first), 1.0, 0.0)
        for first in (0, lanes - 2)
    ]
    arrived = []
    for side in range(2):
        total = row_recv[side].astype(F32)
        for e in range(2):
            total = total + dot(corn_recv[side, e].astype(BF16), back[e].astype(BF16), TN)
        arrived.append(total.astype(BF16))
    back_row, back_lane = iota((4, lanes), 0), iota((4, lanes), 1)
    back_cols = jnp.where(
        back_lane == jnp.where(back_row < 2, back_row, back_row + lanes - 4), 1.0, 0.0
    ).astype(BF16)
    for z in range(ZOUT):
        near = jnp.concatenate([arrived[s][2 * C * z : 2 * C * (z + 1)] for s in range(2)], axis=0)
        for b in range(blocks):
            at = pl.ds((z * blocks + b) * block, block)
            cols = jnp.concatenate([col_recv[0, :, at], col_recv[1, :, at]], axis=0)
            total = local[z, b].reshape(block, lanes) + dot(place[b], near)
            total = total + dot(cols.astype(BF16), back_cols, TN)
            depth_ref[z, pl.ds(b * block, block), :] = total.astype(BF16)

    for copy in copies:
        copy.wait_send()


def mix_kernel(
    widths, pwb_s, lift_s, pw_v, up, depth, feat, out, field, mixed, result, in_sem, out_sem
):
    lanes = feat.shape[3]
    blocks = feat.shape[2] // SUB
    block = C * SUB
    loads = []
    for z in range(ZOUT):
        for b in range(blocks):
            loads.append(
                pltpu.make_async_copy(
                    feat.at[ZOUT + z, :, pl.ds(SUB * b, SUB), :], field.at[z, b], in_sem.at[z, b]
                )
            )
            loads[-1].start()
    width = widths[lax.axis_index("gx")]
    tall = (iota((block, C), 0) // SUB == iota((block, C), 1)).astype(BF16)
    flat = (iota((C, block), 1) // SUB == iota((C, block), 0)).astype(BF16)
    full = dot(dot(tall, pw_v[...]).astype(BF16), flat)
    keep = iota((block, block), 0) % SUB == iota((block, block), 1) % SUB
    full = jnp.where(keep, full, 0.0).astype(BF16)
    for b in range(blocks):
        at = pl.ds(b * block, block)
        cells = jnp.concatenate([depth[z, at, :] for z in range(ZOUT)], axis=1)
        mixed[b] = dot(full, cells).reshape(C, SUB, ZOUT * lanes)
    for load in loads:
        load.wait()
    ups = [
        [up[pl.ds(k * blocks * SUB + b * SUB, SUB), :] for b in range(blocks)] for k in range(3)
    ]
    slot = iota((SUB, lanes), 0)

    def pair(i, carry):
        for b in range(blocks):
            lifted = []
            for h in range(2):
                c = 2 * i + h
                total = lift_s[0, c] * ups[0][b] + lift_s[1, c] * ups[1][b] + lift_s[2, c] * ups[2][b]
                lifted.append(total)
            for z in range(ZOUT):
                values = []
                cells = field[z, b, pl.ds(2 * i, 2)].astype(F32)
                for h in range(2):
                    c = 2 * i + h
                    v = mixed[b, c, :, z * lanes : (z + 1) * lanes] + pwb_s[c]
                    v = cells[h] + jnp.where(v > 0, v, 0.2 * v) + lifted[h]
                    values.append(jnp.where(slot + SUB * b < width, v, 0.0))
                result[z, b, pl.ds(2 * i, 2)] = jnp.stack(values).astype(BF16)
        return carry

    parts = 4
    size = C // parts
    stores = []
    for part in range(parts):
        lax.fori_loop(part * size // 2, (part + 1) * size // 2, pair, 0)
        for z in range(ZOUT):
            for b in range(blocks):
                stores.append(
                    pltpu.make_async_copy(
                        result.at[z, b, pl.ds(part * size, size)],
                        out.at[z, pl.ds(part * size, size), pl.ds(SUB * b, SUB), :],
                        out_sem.at[part, z, b],
                    )
                )
                stores[-1].start()
    for store in stores:
        store.wait()


def shards(feature, widths, dw_weight, dw_bias, pw_weight, pw_bias, lift_weight, coarse):
    nx, ny = lax.axis_size("gx"), lax.axis_size("gy")
    slots, lanes = feature.shape[2], feature.shape[3]
    blocks = slots // SUB
    block = C * SUB
    ncols = coarse.shape[2]
    smem = pl.BlockSpec(memory_space=pltpu.SMEM)
    vmem = pl.BlockSpec(memory_space=pltpu.VMEM)
    anyw = pl.BlockSpec(memory_space=pl.ANY)
    dma = pltpu.SemaphoreType.DMA
    depth, up = pl.pallas_call(
        functools.partial(depth_kernel, nx, ny),
        out_shape=(
            jax.ShapeDtypeStruct((ZOUT, blocks * block, lanes), BF16),
            jax.ShapeDtypeStruct((3 * slots, lanes), F32),
        ),
        in_specs=[smem, smem, smem, vmem, vmem, anyw],
        out_specs=(vmem, vmem),
        scratch_shapes=[
            pltpu.VMEM((ZIN, blocks, C, SUB, lanes), BF16),
            pltpu.VMEM((ZOUT, blocks, C, SUB, lanes), F32),
            pltpu.VMEM((2, ZIN, 2, C, lanes), F32),
            pltpu.VMEM((2, 9, C, lanes), F32),
            pltpu.VMEM((blocks, block, 4 * C), BF16),
            pltpu.VMEM((2, ZIN, (blocks + 2) * SUB, lanes), F32),
            pltpu.VMEM((2, 2, ZOUT * 2 * C, lanes), BF16),
            pltpu.VMEM((ZIN, blocks, SUB, block), F32),
            pltpu.VMEM((2, ZOUT * 2 * C, lanes), BF16),
            pltpu.VMEM((2, ZOUT * 2 * C, lanes), BF16),
            pltpu.VMEM((2, 2, SUB, ZOUT * 2 * C), F32),
            pltpu.VMEM((2, 2, SUB, ZOUT * 2 * C), F32),
            pltpu.VMEM((2, 2, ZOUT * blocks * block), F32),
            pltpu.VMEM((2, 2, ZOUT * blocks * block), F32),
            pltpu.VMEM((SUB, ncols), F32),
            pltpu.VMEM((ny, SUB, ncols), F32),
            dma((ZIN, blocks)),
            dma((2,)), dma((2,)), dma((2, 2)), dma((2, 2)), dma((2,)), dma((2,)),
            dma((ny - 1,)), dma((ny - 1,)),
        ],
        compiler_params=pltpu.CompilerParams(collective_id=0, has_side_effects=True),
        name="depth",
    )(widths, dw_weight, dw_bias, dw_weight, coarse, feature)
    return pl.pallas_call(
        mix_kernel,
        out_shape=jax.ShapeDtypeStruct((ZOUT, C, slots, lanes), BF16),
        in_specs=[smem, smem, smem, vmem, vmem, vmem, anyw],
        out_specs=anyw,
        scratch_shapes=[
            pltpu.VMEM((ZOUT, blocks, C, SUB, lanes), BF16),
            pltpu.VMEM((blocks, C, SUB, ZOUT * lanes), F32),
            pltpu.VMEM((ZOUT, blocks, C, SUB, lanes), BF16),
            dma((ZOUT, blocks)),
            dma((4, ZOUT, blocks)),
        ],
        name="mix",
    )(widths, pw_bias, lift_weight.T, pw_weight, up, depth, feature)


def solution(mesh):
    placed = (P(None, None, "gx", "gy"), P(), P(), P(), P(), P(), P(), P(None, "gy", None))
    return jax.shard_map(
        shards, mesh=mesh, in_specs=placed, out_specs=P(None, None, "gx", "gy"), check_vma=False
    )
```

```python
import functools

import jax
import jax.numpy as jnp
from jax import lax
from jax.experimental import pallas as pl
from jax.experimental.pallas import tpu as pltpu
from jax.sharding import PartitionSpec as P

MESH = pl.DeviceIdType.MESH
XW = 16
ZIN = 6
ZOUT = 2
C = 64
CF = 16
VMEM_LIMIT = 50000 * 1024
SUB = 8
F32 = jnp.float32
BF16 = jnp.bfloat16
HIGH = lax.Precision.HIGHEST
NN = (((1,), (0,)), ((), ()))
NT = (((1,), (1,)), ((), ()))
TN = (((0,), (0,)), ((), ()))


def iota(shape, dim):
    return lax.broadcasted_iota(jnp.int32, shape, dim)


def dot(a, b, dims=NN, precision=None):
    return lax.dot_general(a, b, dims, precision=precision, preferred_element_type=F32)


def tap(dz, dx, dy):
    return 9 * (dz + 1) + 3 * (dx + 1) + (dy + 1)


def block_kernel(
    nx, ny,
    widths_h, dw_h, dwb_h, pw_h, pwb_h, lift_h, coarse_h, feat,
    out,
    widths, dw_s, bias_s, pwb_s, lift_s, dw_v, pw_v, coarse,
    field, local, mixed, base, result, rim, wide, near_w, stage, rim_edge, edge,
    row_send, row_recv, corn_send, corn_recv, col_send, col_recv, own, coarse_all,
    arg_sem, field_sem, row_ssem, row_rsem, corn_ssem, corn_rsem, col_ssem, col_rsem,
    co_ssem, co_rsem, out_sem,
):
    lanes = feat.shape[3]
    blocks = feat.shape[2] // SUB
    block = C * SUB
    gx, gy = lax.axis_index("gx"), lax.axis_index("gy")
    sides = (lax.rem(gx + nx - 1, nx), lax.rem(gx + 1, nx))

    def along(k):
        return lax.rem(gy + k, ny)

    lefts = (along(ny - 1), along(1))

    given = (
        (widths_h, widths), (dw_h, dw_v), (dw_h, dw_s), (coarse_h, coarse), (dwb_h, bias_s),
        (pwb_h, pwb_s), (lift_h, lift_s), (pw_h, pw_v),
    )
    fetch = [pltpu.make_async_copy(a, b, arg_sem.at[i]) for i, (a, b) in enumerate(given)]
    for copy in fetch[:4]:
        copy.start()
    loads = []
    for p in range(ZIN):
        for b in range(blocks):
            loads.append(
                pltpu.make_async_copy(
                    feat.at[p, :, pl.ds(SUB * b, SUB), :], field.at[p, b], field_sem.at[p, b]
                )
            )
            loads[-1].start()

    barrier = pltpu.get_barrier_semaphore()
    for x in sides:
        for y in (gy,) + lefts:
            pl.semaphore_signal(barrier, inc=1, device_id=(x, y), device_id_type=MESH)
    for k in range(1, ny):
        pl.semaphore_signal(barrier, inc=1, device_id=(gx, along(k)), device_id_type=MESH)
    for copy in fetch[4:]:
        copy.start()
    for copy in fetch[:4]:
        copy.wait()
    width = widths[gx]

    def send(src, dst, ssem, rsem, to):
        return pltpu.make_async_remote_copy(
            src_ref=src, dst_ref=dst, send_sem=ssem, recv_sem=rsem, device_id=to,
            device_id_type=MESH,
        )

    rows_out = [
        send(
            row_send.at[s], row_recv.at[1 - s], row_ssem.at[s], row_rsem.at[1 - s], (sides[s], gy)
        )
        for s in range(2)
    ]
    corners_out = [
        send(
            corn_send.at[s, e], corn_recv.at[1 - s, 1 - e], corn_ssem.at[s, e],
            corn_rsem.at[1 - s, 1 - e], (sides[s], lefts[e]),
        )
        for s in range(2) for e in range(2)
    ]
    cols_out = [
        send(col_send.at[e], col_recv.at[1 - e], col_ssem.at[e], col_rsem.at[1 - e], (gx, lefts[e]))
        for e in range(2)
    ]
    coarse_out = [
        send(own, coarse_all.at[gy], co_ssem.at[k - 1], co_rsem.at[k - 1], (gx, along(k)))
        for k in range(1, ny)
    ]
    last = lax.rem(gx, nx // 2 if nx % 2 == 0 else nx) == 0
    soon = jnp.logical_not(last)

    def meet():
        pl.semaphore_wait(barrier, ny - 1 + 6)

    rows = coarse.shape[1]
    own[...] = jnp.zeros_like(own)
    for k in range(3):
        own[pl.ds(k * rows, rows), :] = coarse[k]
    coarse_all[gy] = own[...]

    eye = (iota((C, C), 0) == iota((C, C), 1)).astype(F32)
    by_channel = dot(eye, dw_v[...], NT, HIGH)
    for side, dx in ((1, -1), (0, 1)):
        for dz in (-1, 0, 1):
            for dy in (-1, 0, 1):
                t = tap(dz, dx, dy)
                wide[side, 3 * (dz + 1) + dy + 1] = jnp.broadcast_to(
                    by_channel[:, t : t + 1], (C, lanes)
                )

    half = C // 2
    pick_row = iota((2 * half, half * SUB), 0)
    pick_col = iota((2 * half, half * SUB), 1)
    same = (pick_row % half) == (pick_col // SUB)

    def picks(first, b):
        hit = same & ((pick_col % SUB) + SUB * b == first + pick_row // half)
        return jnp.where(hit, 1.0, 0.0).astype(BF16)

    pick_rim = [picks(0, 0), jnp.concatenate([picks(width - 2, b) for b in range(blocks)], axis=1)]
    lane = iota((C, lanes), 1)
    ends_row, ends_lane = iota((16, lanes), 0), iota((16, lanes), 1)
    ends = [
        jnp.where(
            (ends_row // 2 == 1 - e) & (ends_lane == ends_row % 2 + e * (lanes - 2)), 1.0, 0.0
        ).astype(BF16)
        for e in range(2)
    ]
    for side in (1, 0):
        for p in range(ZIN):
            if side == 1:
                for b in range(blocks):
                    loads[p * blocks + b].wait()
            for h in range(2):
                part = [
                    field[p, b, pl.ds(h * half, half)].reshape(half * SUB, lanes)
                    for b in range(blocks if side == 1 else 1)
                ]
                found = dot(pick_rim[side], jnp.concatenate(part, axis=0) if side == 1 else part[0])
                for r in range(2):
                    rim[side, p, r, pl.ds(h * half, half), :] = found[r * half : (r + 1) * half]
        for z in range(ZOUT):
            for r in range(2):
                sums = [None, None, None]
                for dz in (-1, 0, 1):
                    cells = rim[side, z + 2 + 2 * dz, r]
                    for dy in (-1, 0, 1):
                        term = wide[side, 3 * (dz + 1) + dy + 1] * cells
                        sums[dy + 1] = term if sums[dy + 1] is None else sums[dy + 1] + term
                total = sums[1]
                total = total + jnp.where(lane < lanes - 2, pltpu.roll(sums[2], lanes - 2, 1), 0.0)
                total = total + jnp.where(lane >= 2, pltpu.roll(sums[0], 2, 1), 0.0)
                row_send[side, pl.ds(r * C, C), pl.ds(z * lanes, lanes)] = total.astype(BF16)
                at = pl.ds(z * 2 * C + r * C, C)
                rim_edge[side, 0, at, :] = sums[2].astype(BF16)
                rim_edge[side, 1, at, :] = sums[0].astype(BF16)
        if side == 1:
            @pl.when(soon)
            def _():
                meet()
                rows_out[1].start()
                for copy in coarse_out:
                    copy.start()

        for e in range(2):
            corn_send[side, e] = dot(ends[e], rim_edge[side, e], NT)[:SUB]

    @pl.when(soon)
    def _():
        rows_out[0].start()
        for copy in corners_out:
            copy.start()

    spread = (iota((C, block), 0) == iota((C, block), 1) // SUB).astype(F32)
    by_lane = dot(dw_v[...], spread, NN, HIGH)
    both = jnp.where(
        ((ends_row < 2) & (ends_lane == ends_row))
        | ((ends_row >= 2) & (ends_row < 4) & (ends_lane == ends_row + lanes - 4)),
        1.0, 0.0,
    ).astype(BF16)
    in_block = iota((SUB, block), 1) % SUB
    for p in range(ZIN):
        for b in range(blocks):
            found = dot(both, field[p, b].reshape(block, lanes), NT)[:SUB]
            edge[p, b] = jnp.where(in_block + SUB * b < width, found, 0.0)
    first_two = iota((SUB, block), 0) < 2
    weight = {}
    for dz in (-1, 0, 1):
        for dx in (-1, 0, 1):
            high, low = tap(dz, dx, 1), tap(dz, dx, -1)
            weight[dz, dx] = jnp.where(
                first_two,
                jnp.broadcast_to(by_lane[high : high + 1], (SUB, block)),
                jnp.broadcast_to(by_lane[low : low + 1], (SUB, block)),
            )
    col_send[...] = jnp.zeros_like(col_send)
    for z in range(ZOUT):
        sums = {}
        for dx in (-1, 0, 1):
            for b in range(blocks):
                total = weight[-1, dx] * edge[z, b]
                total = total + weight[0, dx] * edge[z + 2, b]
                sums[dx, b] = total + weight[1, dx] * edge[z + 4, b]
        for b in range(blocks):
            total = sums[0, b]
            total = total + jnp.where(in_block < 6, pltpu.roll(sums[1, b], block - 2, 1), 0.0)
            total = total + jnp.where(in_block >= 2, pltpu.roll(sums[-1, b], 2, 1), 0.0)
            if b + 1 < blocks:
                total = total + jnp.where(in_block >= 6, pltpu.roll(sums[1, b + 1], 6, 1), 0.0)
            if b > 0:
                total = total + jnp.where(
                    in_block < 2, pltpu.roll(sums[-1, b - 1], block - 6, 1), 0.0
                )
            at = pl.ds(2 * (z * blocks + b), 2)
            col_send[0, at, :] = total[0:2]
            col_send[1, at, :] = total[2:4]
    @pl.when(soon)
    def _():
        for copy in cols_out:
            copy.start()

    for copy in fetch[4:]:
        copy.wait()
    stage[...] = jnp.zeros_like(stage)
    slot = iota((2, SUB, lanes), 1)
    line = iota((blocks * SUB, lanes), 1)

    def taps(i, carry):
        c0 = 2 * i
        for p in range(ZIN):
            for b in range(blocks):
                cells = field[p, b, pl.ds(c0, 2)].astype(F32)
                if b > 0:
                    cells = jnp.where(slot + SUB * b < width, cells, 0.0)
                for h in range(2):
                    stage[h, p, pl.ds(SUB * (b + 1), SUB), :] = cells[h]
        for z in range(ZOUT):
            totals = []
            for h in range(2):
                sums = [None, None, None]
                for dz in (-1, 0, 1):
                    for dx in (-1, 0, 1):
                        cells = stage[h, z + 2 + 2 * dz, pl.ds(SUB + 2 * dx, SUB * blocks), :]
                        for dy in (-1, 0, 1):
                            term = dw_s[tap(dz, dx, dy), c0 + h] * cells
                            sums[dy + 1] = term if sums[dy + 1] is None else sums[dy + 1] + term
                total = sums[1] + bias_s[c0 + h]
                total = total + jnp.where(line < lanes - 2, pltpu.roll(sums[2], lanes - 2, 1), 0.0)
                total = total + jnp.where(line >= 2, pltpu.roll(sums[0], 2, 1), 0.0)
                totals.append(total)
            for b in range(blocks):
                pair = jnp.stack([total[SUB * b : SUB * (b + 1)] for total in totals])
                local[b, pl.ds(c0, 2), :, pl.ds(z * lanes, lanes)] = pair.astype(BF16)
        return carry

    lax.fori_loop(0, C // 2, taps, 0)

    tall = (iota((block, C), 0) // SUB == iota((block, C), 1)).astype(BF16)
    wide_mix = dot(tall, pw_v[...]).astype(BF16)
    flat = (iota((C, block), 1) // SUB == iota((C, block), 0)).astype(BF16)
    keep = iota((block, block), 0) % SUB == iota((block, block), 1) % SUB
    full = jnp.where(keep, dot(wide_mix, flat), 0.0).astype(BF16)
    for b in range(blocks):
        mixed[b] = dot(full, local[b].reshape(block, ZOUT * lanes)).reshape(C, SUB, ZOUT * lanes)
    four = (iota((C, 4 * C), 1) % C == iota((C, 4 * C), 0)).astype(BF16)
    arriving = dot(wide_mix, four)
    put_row, put_col = iota((block, 4 * C), 0), iota((block, 4 * C), 1)
    target = jnp.where(put_col < 2 * C, put_col // C, width - 4 + put_col // C)
    for b in range(blocks):
        hit = (put_row % SUB) + SUB * b == target
        near_w[b] = jnp.where(hit, arriving, 0.0).astype(BF16)

    @pl.when(last)
    def _():
        meet()
        for copy in rows_out[::-1] + coarse_out + corners_out + cols_out:
            copy.start()

    for copy in coarse_out:
        copy.wait_recv()
    start = jnp.int32(0)
    for d in range(nx):
        start = start + jnp.where(d < gx, widths[d], 0)
    ncols = coarse_all.shape[2]
    held = coarse_all[...].reshape(ny * SUB, ncols)
    column = (
        iota((ncols, lanes), 0) == gy * (lanes // CF) + iota((ncols, lanes), 1) // CF
    ).astype(F32)
    count = blocks * SUB
    up_row, up_col = iota((3 * count, ny * SUB), 0), iota((3 * count, ny * SUB), 1)
    cell = start + up_row % count
    cell = jnp.where(cell >= XW * nx, cell - XW * nx, cell) // CF
    hit = (up_col // SUB == cell // rows) & (up_col % SUB == (up_row // count) * rows + cell % rows)
    along_y = dot(held, column, NN, HIGH)
    up = dot(jnp.where(hit, 1.0, 0.0), along_y, NN, HIGH)
    ups = [
        [up[k * count + b * SUB : k * count + (b + 1) * SUB] for b in range(blocks)] for k in range(3)
    ]

    def ready(i, carry):
        for b in range(blocks):
            lifted = []
            for h in range(2):
                c = 2 * i + h
                total = lift_s[0, c] * ups[0][b] + lift_s[1, c] * ups[1][b]
                lifted.append(total + lift_s[2, c] * ups[2][b])
            for z in range(ZOUT):
                at = pl.ds(z * lanes, lanes)
                cells = field[ZOUT + z, b, pl.ds(2 * i, 2)].astype(F32)
                for h in range(2):
                    c = 2 * i + h
                    base[b, c, :, at] = cells[h] + lifted[h]
                    mixed[b, c, :, at] = mixed[b, c, :, at] + pwb_s[c]
        return carry

    lax.fori_loop(0, C // 2, ready, 0)

    back_row, back_lane = iota((SUB, lanes), 0), iota((SUB, lanes), 1)
    back = jnp.where(
        (back_row < 4)
        & (back_lane == jnp.where(back_row < 2, back_row, back_row + lanes - 4)),
        1.0, 0.0,
    ).astype(BF16)
    ends_k, ends_l = iota((32, ZOUT * lanes), 0), iota((32, ZOUT * lanes), 1)
    spot = ends_l % lanes - (ends_k // 16) * (lanes - 2)

    for copy in corners_out + cols_out:
        copy.wait_recv()
    cols = jnp.concatenate([col_recv[0], col_recv[1]], axis=0).astype(BF16)
    mixed_cols = dot(full, cols, NT).astype(BF16)
    corners = [
        dot((corn_recv[side, 0] + corn_recv[side, 1]).astype(BF16), back, TN) for side in range(2)
    ]
    for copy in rows_out:
        copy.wait_recv()
    arrived = []
    for side in range(2):
        parts = [
            row_recv[side, :, pl.ds(z * lanes, lanes)].astype(F32)
            + corners[side][2 * C * z : 2 * C * (z + 1)]
            for z in range(ZOUT)
        ]
        arrived.append(jnp.concatenate(parts, axis=1).astype(BF16))
    stores = []
    for b in range(blocks):
        at_lane = (ends_k % 16) // 2 == (ends_l // lanes) * blocks + b
        pick = jnp.where(at_lane & (spot == ends_k % 2), 1.0, 0.0).astype(BF16)
        right = jnp.concatenate(arrived + [pick], axis=0)
        row_id = iota((block, ZOUT * lanes), 0) % SUB + SUB * b
        v = dot(jnp.concatenate([near_w[b], mixed_cols], axis=1), right)
        v = v + mixed[b].reshape(block, ZOUT * lanes)
        v = base[b].reshape(block, ZOUT * lanes) + jnp.where(v > 0, v, 0.2 * v)
        v = jnp.where(row_id < width, v, 0.0).astype(BF16)
        for z in range(ZOUT):
            result[z, b] = v[:, z * lanes : (z + 1) * lanes].reshape(C, SUB, lanes)
            stores.append(
                pltpu.make_async_copy(
                    result.at[z, b], out.at[z, :, pl.ds(SUB * b, SUB), :], out_sem.at[z, b]
                )
            )
            stores[-1].start()

    for copy in rows_out + corners_out + cols_out + coarse_out:
        copy.wait_send()
    for store in stores:
        store.wait()


def shards(feature, widths, dw_weight, dw_bias, pw_weight, pw_bias, lift_weight, coarse):
    nx, ny = lax.axis_size("gx"), lax.axis_size("gy")
    slots, lanes = feature.shape[2], feature.shape[3]
    blocks = slots // SUB
    block = C * SUB
    both = ZOUT * lanes
    ncols = coarse.shape[2]
    lift = lift_weight.T
    dma = pltpu.SemaphoreType.DMA
    vmem, smem = pltpu.VMEM, pltpu.SMEM
    return pl.pallas_call(
        functools.partial(block_kernel, nx, ny),
        out_shape=jax.ShapeDtypeStruct((ZOUT, C, slots, lanes), BF16),
        in_specs=[pl.BlockSpec(memory_space=pltpu.HBM)] * 8,
        out_specs=pl.BlockSpec(memory_space=pl.ANY),
        scratch_shapes=[
            smem(widths.shape, jnp.int32),
            smem(dw_weight.shape, F32),
            smem(dw_bias.shape, F32),
            smem(pw_bias.shape, F32),
            smem(lift.shape, F32),
            vmem(dw_weight.shape, F32),
            vmem(pw_weight.shape, BF16),
            vmem(coarse.shape, F32),
            vmem((ZIN, blocks, C, SUB, lanes), BF16),
            vmem((blocks, C, SUB, both), BF16),
            vmem((blocks, C, SUB, both), F32),
            vmem((blocks, C, SUB, both), F32),
            vmem((ZOUT, blocks, C, SUB, lanes), BF16),
            vmem((2, ZIN, 2, C, lanes), F32),
            vmem((2, 9, C, lanes), F32),
            vmem((blocks, block, 4 * C), BF16),
            vmem((2, ZIN, (blocks + 2) * SUB, lanes), F32),
            vmem((2, 2, ZOUT * 2 * C, lanes), BF16),
            vmem((ZIN, blocks, SUB, block), F32),
            vmem((2, 2 * C, both), BF16),
            vmem((2, 2 * C, both), BF16),
            vmem((2, 2, SUB, ZOUT * 2 * C), F32),
            vmem((2, 2, SUB, ZOUT * 2 * C), F32),
            vmem((2, 16, block), F32),
            vmem((2, 16, block), F32),
            vmem((SUB, ncols), F32),
            vmem((ny, SUB, ncols), F32),
            dma((8,)),
            dma((ZIN, blocks)),
            dma((2,)), dma((2,)), dma((2, 2)), dma((2, 2)), dma((2,)), dma((2,)),
            dma((ny - 1,)), dma((ny - 1,)),
            dma((ZOUT, blocks)),
        ],
        compiler_params=pltpu.CompilerParams(
            collective_id=0, has_side_effects=True, vmem_limit_bytes=VMEM_LIMIT
        ),
        name="block",
    )(
        *[
            pltpu.with_memory_space_constraint(a, pltpu.HBM)
            for a in (widths, dw_weight, dw_bias, pw_weight, pw_bias, lift, coarse, feature)
        ]
    )


def solution(mesh):
    placed = (P(None, None, "gx", "gy"), P(), P(), P(), P(), P(), P(), P(None, "gy", None))
    return jax.shard_map(
        shards, mesh=mesh, in_specs=placed, out_specs=P(None, None, "gx", "gy"), check_vma=False
    )
```

```python
import functools

import jax
import jax.numpy as jnp
from jax import lax
from jax.experimental import pallas as pl
from jax.experimental.pallas import tpu as pltpu
from jax.sharding import PartitionSpec as P

MESH = pl.DeviceIdType.MESH
XW = 16
ZIN = 6
ZOUT = 2
C = 64
CF = 16
VMEM_LIMIT = 50000 * 1024
SUB = 8
F32 = jnp.float32
BF16 = jnp.bfloat16
HIGH = lax.Precision.HIGHEST
NN = (((1,), (0,)), ((), ()))
NT = (((1,), (1,)), ((), ()))
TN = (((0,), (0,)), ((), ()))


def iota(shape, dim):
    return lax.broadcasted_iota(jnp.int32, shape, dim)


def dot(a, b, dims=NN, precision=None):
    return lax.dot_general(a, b, dims, precision=precision, preferred_element_type=F32)


def tap(dz, dx, dy):
    return 9 * (dz + 1) + 3 * (dx + 1) + (dy + 1)


def block_kernel(
    nx, ny,
    widths_h, dw_h, dwb_h, pw_h, pwb_h, lift_h, coarse_h, feat,
    out,
    widths, dw_s, bias_s, pwb_s, lift_s, dw_v, pw_v, coarse,
    field, local, mixed, base, result, rim, wide, near_w, stage, rim_edge, edge,
    row_send, row_recv, corn_send, corn_recv, col_send, col_recv, own, coarse_all,
    arg_sem, field_sem, row_ssem, row_rsem, corn_ssem, corn_rsem, col_ssem, col_rsem,
    co_ssem, co_rsem, out_sem, here,
):
    lanes = feat.shape[3]
    blocks = feat.shape[2] // SUB
    block = C * SUB
    gx, gy = lax.axis_index("gx"), lax.axis_index("gy")
    sides = (lax.rem(gx + nx - 1, nx), lax.rem(gx + 1, nx))

    def along(k):
        return lax.rem(gy + k, ny)

    lefts = (along(ny - 1), along(1))

    given = (
        (widths_h, widths), (dw_h, dw_v), (dw_h, dw_s), (coarse_h, coarse), (dwb_h, bias_s),
        (pwb_h, pwb_s), (lift_h, lift_s), (pw_h, pw_v),
    )
    fetch = [pltpu.make_async_copy(a, b, arg_sem.at[i]) for i, (a, b) in enumerate(given)]
    for copy in fetch[:4]:
        copy.start()
    loads = []
    for p in range(ZIN):
        for b in range(blocks):
            loads.append(
                pltpu.make_async_copy(
                    feat.at[p, :, pl.ds(SUB * b, SUB), :], field.at[p, b], field_sem.at[p, b]
                )
            )
            loads[-1].start()

    barrier = pltpu.get_barrier_semaphore()
    span = nx // 2 if nx % 2 == 0 else nx
    first = lax.rem(gx, span) == 0
    for y in (gy,) + lefts:
        pl.semaphore_signal(barrier, inc=1, device_id=(sides[0], y), device_id_type=MESH)

    @pl.when(lax.rem(gx, span) != span - 1)
    def _():
        for y in (gy,) + lefts:
            pl.semaphore_signal(barrier, inc=1, device_id=(sides[1], y), device_id_type=MESH)

    for k in range(1, ny):
        pl.semaphore_signal(barrier, inc=1, device_id=(gx, along(k)), device_id_type=MESH)
    for copy in fetch[4:]:
        copy.start()
    for copy in fetch[:4]:
        copy.wait()
    width = widths[gx]

    def send(src, dst, ssem, rsem, to):
        return pltpu.make_async_remote_copy(
            src_ref=src, dst_ref=dst, send_sem=ssem, recv_sem=rsem, device_id=to,
            device_id_type=MESH,
        )

    rows_out = [
        send(
            row_send.at[s], row_recv.at[1 - s], row_ssem.at[s], row_rsem.at[1 - s], (sides[s], gy)
        )
        for s in range(2)
    ]
    corners_out = [
        send(
            corn_send.at[s, e], corn_recv.at[1 - s, 1 - e], corn_ssem.at[s, e],
            corn_rsem.at[1 - s, 1 - e], (sides[s], lefts[e]),
        )
        for s in range(2) for e in range(2)
    ]
    cols_out = [
        send(col_send.at[e], col_recv.at[1 - e], col_ssem.at[e], col_rsem.at[1 - e], (gx, lefts[e]))
        for e in range(2)
    ]
    coarse_out = [
        send(own, coarse_all.at[gy], co_ssem.at[k - 1], co_rsem.at[k - 1], (gx, along(k)))
        for k in range(1, ny)
    ]
    rows = coarse.shape[1]
    own[...] = jnp.zeros_like(own)
    for k in range(3):
        own[pl.ds(k * rows, rows), :] = coarse[k]
    coarse_all[gy] = own[...]

    eye = (iota((C, C), 0) == iota((C, C), 1)).astype(F32)
    by_channel = dot(eye, dw_v[...], NT, HIGH)
    for side, dx in ((1, -1), (0, 1)):
        for dz in (-1, 0, 1):
            for dy in (-1, 0, 1):
                t = tap(dz, dx, dy)
                wide[side, 3 * (dz + 1) + dy + 1] = jnp.broadcast_to(
                    by_channel[:, t : t + 1], (C, lanes)
                )

    half = C // 2
    pick_row = iota((2 * half, half * SUB), 0)
    pick_col = iota((2 * half, half * SUB), 1)
    same = (pick_row % half) == (pick_col // SUB)

    def picks(first, b):
        hit = same & ((pick_col % SUB) + SUB * b == first + pick_row // half)
        return jnp.where(hit, 1.0, 0.0).astype(BF16)

    pick_rim = [picks(0, 0), jnp.concatenate([picks(width - 2, b) for b in range(blocks)], axis=1)]
    lane = iota((C, lanes), 1)
    ends_row, ends_lane = iota((16, lanes), 0), iota((16, lanes), 1)
    ends = [
        jnp.where(
            (ends_row // 2 == 1 - e) & (ends_lane == ends_row % 2 + e * (lanes - 2)), 1.0, 0.0
        ).astype(BF16)
        for e in range(2)
    ]
    for side in (1, 0):
        for p in range(ZIN):
            if side == 1:
                for b in range(blocks):
                    loads[p * blocks + b].wait()
            for h in range(2):
                part = [
                    field[p, b, pl.ds(h * half, half)].reshape(half * SUB, lanes)
                    for b in range(blocks if side == 1 else 1)
                ]
                found = dot(pick_rim[side], jnp.concatenate(part, axis=0) if side == 1 else part[0])
                for r in range(2):
                    rim[side, p, r, pl.ds(h * half, half), :] = found[r * half : (r + 1) * half]
        for z in range(ZOUT):
            for r in range(2):
                sums = [None, None, None]
                for dz in (-1, 0, 1):
                    cells = rim[side, z + 2 + 2 * dz, r]
                    for dy in (-1, 0, 1):
                        term = wide[side, 3 * (dz + 1) + dy + 1] * cells
                        sums[dy + 1] = term if sums[dy + 1] is None else sums[dy + 1] + term
                total = sums[1]
                total = total + jnp.where(lane < lanes - 2, pltpu.roll(sums[2], lanes - 2, 1), 0.0)
                total = total + jnp.where(lane >= 2, pltpu.roll(sums[0], 2, 1), 0.0)
                row_send[side, pl.ds(r * C, C), pl.ds(z * lanes, lanes)] = total.astype(BF16)
                at = pl.ds(z * 2 * C + r * C, C)
                rim_edge[side, 0, at, :] = sums[2].astype(BF16)
                rim_edge[side, 1, at, :] = sums[0].astype(BF16)
        if side == 1:
            pl.semaphore_wait(barrier, jnp.where(first, ny - 1 + 3, ny - 1 + 6))
            rows_out[1].start()

            @pl.when(lax.rem(gx, span) == span - 1)
            def _():
                for y in (gy,) + lefts:
                    pl.semaphore_signal(here, inc=1, device_id=(sides[1], y), device_id_type=MESH)


        for e in range(2):
            corn_send[side, e] = dot(ends[e], rim_edge[side, e], NT)[:SUB]

    for copy in corners_out[2:]:
        copy.start()

    @pl.when(jnp.logical_not(first))
    def _():
        rows_out[0].start()
        for copy in corners_out[:2]:
            copy.start()

    for copy in coarse_out:
        copy.start()

    spread = (iota((C, block), 0) == iota((C, block), 1) // SUB).astype(F32)
    by_lane = dot(dw_v[...], spread, NN, HIGH)
    both = jnp.where(
        ((ends_row < 2) & (ends_lane == ends_row))
        | ((ends_row >= 2) & (ends_row < 4) & (ends_lane == ends_row + lanes - 4)),
        1.0, 0.0,
    ).astype(BF16)
    in_block = iota((SUB, block), 1) % SUB
    for p in range(ZIN):
        for b in range(blocks):
            found = dot(both, field[p, b].reshape(block, lanes), NT)[:SUB]
            edge[p, b] = jnp.where(in_block + SUB * b < width, found, 0.0)
    first_two = iota((SUB, block), 0) < 2
    weight = {}
    for dz in (-1, 0, 1):
        for dx in (-1, 0, 1):
            high, low = tap(dz, dx, 1), tap(dz, dx, -1)
            weight[dz, dx] = jnp.where(
                first_two,
                jnp.broadcast_to(by_lane[high : high + 1], (SUB, block)),
                jnp.broadcast_to(by_lane[low : low + 1], (SUB, block)),
            )
    col_send[...] = jnp.zeros_like(col_send)
    for z in range(ZOUT):
        sums = {}
        for dx in (-1, 0, 1):
            for b in range(blocks):
                total = weight[-1, dx] * edge[z, b]
                total = total + weight[0, dx] * edge[z + 2, b]
                sums[dx, b] = total + weight[1, dx] * edge[z + 4, b]
        for b in range(blocks):
            total = sums[0, b]
            total = total + jnp.where(in_block < 6, pltpu.roll(sums[1, b], block - 2, 1), 0.0)
            total = total + jnp.where(in_block >= 2, pltpu.roll(sums[-1, b], 2, 1), 0.0)
            if b + 1 < blocks:
                total = total + jnp.where(in_block >= 6, pltpu.roll(sums[1, b + 1], 6, 1), 0.0)
            if b > 0:
                total = total + jnp.where(
                    in_block < 2, pltpu.roll(sums[-1, b - 1], block - 6, 1), 0.0
                )
            at = pl.ds(2 * (z * blocks + b), 2)
            col_send[0, at, :] = total[0:2]
            col_send[1, at, :] = total[2:4]
    for copy in cols_out:
        copy.start()

    for copy in fetch[4:]:
        copy.wait()
    stage[...] = jnp.zeros_like(stage)
    slot = iota((2, SUB, lanes), 1)
    line = iota((blocks * SUB, lanes), 1)

    def taps(i, carry):
        c0 = 2 * i
        for p in range(ZIN):
            for b in range(blocks):
                cells = field[p, b, pl.ds(c0, 2)].astype(F32)
                if b > 0:
                    cells = jnp.where(slot + SUB * b < width, cells, 0.0)
                for h in range(2):
                    stage[h, p, pl.ds(SUB * (b + 1), SUB), :] = cells[h]
        for z in range(ZOUT):
            totals = []
            for h in range(2):
                sums = [None, None, None]
                for dz in (-1, 0, 1):
                    for dx in (-1, 0, 1):
                        cells = stage[h, z + 2 + 2 * dz, pl.ds(SUB + 2 * dx, SUB * blocks), :]
                        for dy in (-1, 0, 1):
                            term = dw_s[tap(dz, dx, dy), c0 + h] * cells
                            sums[dy + 1] = term if sums[dy + 1] is None else sums[dy + 1] + term
                total = sums[1] + bias_s[c0 + h]
                total = total + jnp.where(line < lanes - 2, pltpu.roll(sums[2], lanes - 2, 1), 0.0)
                total = total + jnp.where(line >= 2, pltpu.roll(sums[0], 2, 1), 0.0)
                totals.append(total)
            for b in range(blocks):
                pair = jnp.stack([total[SUB * b : SUB * (b + 1)] for total in totals])
                local[b, pl.ds(c0, 2), :, pl.ds(z * lanes, lanes)] = pair.astype(BF16)
        return carry

    lax.fori_loop(0, C // 2, taps, 0)

    tall = (iota((block, C), 0) // SUB == iota((block, C), 1)).astype(BF16)
    wide_mix = dot(tall, pw_v[...]).astype(BF16)
    flat = (iota((C, block), 1) // SUB == iota((C, block), 0)).astype(BF16)
    keep = iota((block, block), 0) % SUB == iota((block, block), 1) % SUB
    full = jnp.where(keep, dot(wide_mix, flat), 0.0).astype(BF16)
    for b in range(blocks):
        mixed[b] = dot(full, local[b].reshape(block, ZOUT * lanes)).reshape(C, SUB, ZOUT * lanes)
    four = (iota((C, 4 * C), 1) % C == iota((C, 4 * C), 0)).astype(BF16)
    arriving = dot(wide_mix, four)
    put_row, put_col = iota((block, 4 * C), 0), iota((block, 4 * C), 1)
    target = jnp.where(put_col < 2 * C, put_col // C, width - 4 + put_col // C)
    for b in range(blocks):
        hit = (put_row % SUB) + SUB * b == target
        near_w[b] = jnp.where(hit, arriving, 0.0).astype(BF16)

    for copy in coarse_out:
        copy.wait_recv()
    start = jnp.int32(0)
    for d in range(nx):
        start = start + jnp.where(d < gx, widths[d], 0)
    ncols = coarse_all.shape[2]
    held = coarse_all[...].reshape(ny * SUB, ncols)
    column = (
        iota((ncols, lanes), 0) == gy * (lanes // CF) + iota((ncols, lanes), 1) // CF
    ).astype(F32)
    count = blocks * SUB
    up_row, up_col = iota((3 * count, ny * SUB), 0), iota((3 * count, ny * SUB), 1)
    cell = start + up_row % count
    cell = jnp.where(cell >= XW * nx, cell - XW * nx, cell) // CF
    hit = (up_col // SUB == cell // rows) & (up_col % SUB == (up_row // count) * rows + cell % rows)
    along_y = dot(held, column, NN, HIGH)
    up = dot(jnp.where(hit, 1.0, 0.0), along_y, NN, HIGH)
    ups = [
        [up[k * count + b * SUB : k * count + (b + 1) * SUB] for b in range(blocks)] for k in range(3)
    ]

    def ready(i, carry):
        for b in range(blocks):
            lifted = []
            for h in range(2):
                c = 2 * i + h
                total = lift_s[0, c] * ups[0][b] + lift_s[1, c] * ups[1][b]
                lifted.append(total + lift_s[2, c] * ups[2][b])
            for z in range(ZOUT):
                at = pl.ds(z * lanes, lanes)
                cells = field[ZOUT + z, b, pl.ds(2 * i, 2)].astype(F32)
                for h in range(2):
                    c = 2 * i + h
                    base[b, c, :, at] = cells[h] + lifted[h]
                    mixed[b, c, :, at] = mixed[b, c, :, at] + pwb_s[c]
        return carry

    lax.fori_loop(0, C // 2, ready, 0)

    back_row, back_lane = iota((SUB, lanes), 0), iota((SUB, lanes), 1)
    back = jnp.where(
        (back_row < 4)
        & (back_lane == jnp.where(back_row < 2, back_row, back_row + lanes - 4)),
        1.0, 0.0,
    ).astype(BF16)
    ends_k, ends_l = iota((32, ZOUT * lanes), 0), iota((32, ZOUT * lanes), 1)
    spot = ends_l % lanes - (ends_k // 16) * (lanes - 2)

    @pl.when(first)
    def _():
        pl.semaphore_wait(here, 3)
        rows_out[0].start()
        for copy in corners_out[:2]:
            copy.start()

    for copy in corners_out + cols_out:
        copy.wait_recv()
    cols = jnp.concatenate([col_recv[0], col_recv[1]], axis=0).astype(BF16)
    mixed_cols = dot(full, cols, NT).astype(BF16)
    corners = [
        dot((corn_recv[side, 0] + corn_recv[side, 1]).astype(BF16), back, TN) for side in range(2)
    ]
    for copy in rows_out:
        copy.wait_recv()
    arrived = []
    for side in range(2):
        parts = [
            row_recv[side, :, pl.ds(z * lanes, lanes)].astype(F32)
            + corners[side][2 * C * z : 2 * C * (z + 1)]
            for z in range(ZOUT)
        ]
        arrived.append(jnp.concatenate(parts, axis=1).astype(BF16))
    stores = []
    for b in range(blocks):
        at_lane = (ends_k % 16) // 2 == (ends_l // lanes) * blocks + b
        pick = jnp.where(at_lane & (spot == ends_k % 2), 1.0, 0.0).astype(BF16)
        right = jnp.concatenate(arrived + [pick], axis=0)
        row_id = iota((block, ZOUT * lanes), 0) % SUB + SUB * b
        v = dot(jnp.concatenate([near_w[b], mixed_cols], axis=1), right)
        v = v + mixed[b].reshape(block, ZOUT * lanes)
        v = base[b].reshape(block, ZOUT * lanes) + jnp.where(v > 0, v, 0.2 * v)
        v = jnp.where(row_id < width, v, 0.0).astype(BF16)
        for z in range(ZOUT):
            result[z, b] = v[:, z * lanes : (z + 1) * lanes].reshape(C, SUB, lanes)
            stores.append(
                pltpu.make_async_copy(
                    result.at[z, b], out.at[z, :, pl.ds(SUB * b, SUB), :], out_sem.at[z, b]
                )
            )
            stores[-1].start()

    for copy in rows_out + corners_out + cols_out + coarse_out:
        copy.wait_send()
    for store in stores:
        store.wait()


def shards(feature, widths, dw_weight, dw_bias, pw_weight, pw_bias, lift_weight, coarse):
    nx, ny = lax.axis_size("gx"), lax.axis_size("gy")
    slots, lanes = feature.shape[2], feature.shape[3]
    blocks = slots // SUB
    block = C * SUB
    both = ZOUT * lanes
    ncols = coarse.shape[2]
    lift = lift_weight.T
    dma = pltpu.SemaphoreType.DMA
    vmem, smem = pltpu.VMEM, pltpu.SMEM
    return pl.pallas_call(
        functools.partial(block_kernel, nx, ny),
        out_shape=jax.ShapeDtypeStruct((ZOUT, C, slots, lanes), BF16),
        in_specs=[pl.BlockSpec(memory_space=pltpu.HBM)] * 8,
        out_specs=pl.BlockSpec(memory_space=pl.ANY),
        scratch_shapes=[
            smem(widths.shape, jnp.int32),
            smem(dw_weight.shape, F32),
            smem(dw_bias.shape, F32),
            smem(pw_bias.shape, F32),
            smem(lift.shape, F32),
            vmem(dw_weight.shape, F32),
            vmem(pw_weight.shape, BF16),
            vmem(coarse.shape, F32),
            vmem((ZIN, blocks, C, SUB, lanes), BF16),
            vmem((blocks, C, SUB, both), BF16),
            vmem((blocks, C, SUB, both), F32),
            vmem((blocks, C, SUB, both), F32),
            vmem((ZOUT, blocks, C, SUB, lanes), BF16),
            vmem((2, ZIN, 2, C, lanes), F32),
            vmem((2, 9, C, lanes), F32),
            vmem((blocks, block, 4 * C), BF16),
            vmem((2, ZIN, (blocks + 2) * SUB, lanes), F32),
            vmem((2, 2, ZOUT * 2 * C, lanes), BF16),
            vmem((ZIN, blocks, SUB, block), F32),
            vmem((2, 2 * C, both), BF16),
            vmem((2, 2 * C, both), BF16),
            vmem((2, 2, SUB, ZOUT * 2 * C), F32),
            vmem((2, 2, SUB, ZOUT * 2 * C), F32),
            vmem((2, 16, block), F32),
            vmem((2, 16, block), F32),
            vmem((SUB, ncols), F32),
            vmem((ny, SUB, ncols), F32),
            dma((8,)),
            dma((ZIN, blocks)),
            dma((2,)), dma((2,)), dma((2, 2)), dma((2, 2)), dma((2,)), dma((2,)),
            dma((ny - 1,)), dma((ny - 1,)),
            dma((ZOUT, blocks)),
            pltpu.SemaphoreType.REGULAR,
        ],
        compiler_params=pltpu.CompilerParams(
            collective_id=0, has_side_effects=True, vmem_limit_bytes=VMEM_LIMIT
        ),
        name="block",
    )(
        *[
            pltpu.with_memory_space_constraint(a, pltpu.HBM)
            for a in (widths, dw_weight, dw_bias, pw_weight, pw_bias, lift, coarse, feature)
        ]
    )


def solution(mesh):
    placed = (P(None, None, "gx", "gy"), P(), P(), P(), P(), P(), P(), P(None, "gy", None))
    return jax.shard_map(
        shards, mesh=mesh, in_specs=placed, out_specs=P(None, None, "gx", "gy"), check_vma=False
    )
```

```python
import functools

import jax
import jax.numpy as jnp
from jax import lax
from jax.experimental import pallas as pl
from jax.experimental.pallas import tpu as pltpu
from jax.sharding import PartitionSpec as P

MESH = pl.DeviceIdType.MESH
XW = 16
ZIN = 6
ZOUT = 2
C = 64
CF = 16
VMEM_LIMIT = 50000 * 1024
SUB = 8
F32 = jnp.float32
BF16 = jnp.bfloat16
HIGH = lax.Precision.HIGHEST
NN = (((1,), (0,)), ((), ()))
NT = (((1,), (1,)), ((), ()))
TN = (((0,), (0,)), ((), ()))


def iota(shape, dim):
    return lax.broadcasted_iota(jnp.int32, shape, dim)


def dot(a, b, dims=NN, precision=None):
    return lax.dot_general(a, b, dims, precision=precision, preferred_element_type=F32)


def tap(dz, dx, dy):
    return 9 * (dz + 1) + 3 * (dx + 1) + (dy + 1)


def block_kernel(
    nx, ny,
    widths_h, dw_h, dwb_h, pw_h, pwb_h, lift_h, coarse_h, feat,
    out,
    widths, dw_s, bias_s, pwb_s, lift_s, dw_v, pw_v, coarse,
    field, local, mixed, base, result, rim, wide, near_w, stage, rim_edge, edge,
    row_send, row_recv, corn_send, corn_recv, col_send, col_recv, own, coarse_all,
    arg_sem, field_sem, row_ssem, row_rsem, corn_ssem, corn_rsem, col_ssem, col_rsem,
    co_ssem, co_rsem, out_sem, here,
):
    lanes = feat.shape[3]
    blocks = feat.shape[2] // SUB
    block = C * SUB
    gx, gy = lax.axis_index("gx"), lax.axis_index("gy")
    sides = (lax.rem(gx + nx - 1, nx), lax.rem(gx + 1, nx))

    def along(k):
        return lax.rem(gy + k, ny)

    lefts = (along(ny - 1), along(1))

    given = (
        (widths_h, widths), (dw_h, dw_v), (dw_h, dw_s), (coarse_h, coarse), (dwb_h, bias_s),
        (pwb_h, pwb_s), (lift_h, lift_s), (pw_h, pw_v),
    )
    fetch = [pltpu.make_async_copy(a, b, arg_sem.at[i]) for i, (a, b) in enumerate(given)]
    for copy in fetch[:4]:
        copy.start()
    planes = [[z + 2 * k for k in range(3)] for z in range(ZOUT)]
    loads = {}
    for p in planes[0] + planes[1]:
        for b in range(blocks):
            loads[p, b] = pltpu.make_async_copy(
                feat.at[p, :, pl.ds(SUB * b, SUB), :], field.at[p, b], field_sem.at[p, b]
            )
            loads[p, b].start()

    barrier = pltpu.get_barrier_semaphore()
    span = nx // 2 if nx % 2 == 0 else nx
    first = lax.rem(gx, span) == 0
    for y in (gy,) + lefts:
        pl.semaphore_signal(barrier, inc=1, device_id=(sides[0], y), device_id_type=MESH)

    @pl.when(lax.rem(gx, span) != span - 1)
    def _():
        for y in (gy,) + lefts:
            pl.semaphore_signal(barrier, inc=1, device_id=(sides[1], y), device_id_type=MESH)

    for k in range(1, ny):
        pl.semaphore_signal(barrier, inc=1, device_id=(gx, along(k)), device_id_type=MESH)
    for copy in fetch[4:]:
        copy.start()
    for copy in fetch[:4]:
        copy.wait()
    width = widths[gx]

    def send(src, dst, ssem, rsem, to):
        return pltpu.make_async_remote_copy(
            src_ref=src, dst_ref=dst, send_sem=ssem, recv_sem=rsem, device_id=to,
            device_id_type=MESH,
        )

    rows_out = [
        send(
            row_send.at[s, z], row_recv.at[1 - s, z], row_ssem.at[s, z], row_rsem.at[1 - s, z],
            (sides[s], gy),
        )
        for s in range(2) for z in range(ZOUT)
    ]
    corners_out = [
        send(
            corn_send.at[s, e], corn_recv.at[1 - s, 1 - e], corn_ssem.at[s, e],
            corn_rsem.at[1 - s, 1 - e], (sides[s], lefts[e]),
        )
        for s in range(2) for e in range(2)
    ]
    cols_out = [
        send(col_send.at[e], col_recv.at[1 - e], col_ssem.at[e], col_rsem.at[1 - e], (gx, lefts[e]))
        for e in range(2)
    ]
    coarse_out = [
        send(own, coarse_all.at[gy], co_ssem.at[k - 1], co_rsem.at[k - 1], (gx, along(k)))
        for k in range(1, ny)
    ]
    rows = coarse.shape[1]
    own[...] = jnp.zeros_like(own)
    for k in range(3):
        own[pl.ds(k * rows, rows), :] = coarse[k]
    coarse_all[gy] = own[...]

    eye = (iota((C, C), 0) == iota((C, C), 1)).astype(F32)
    by_channel = dot(eye, dw_v[...], NT, HIGH)
    for side, dx in ((1, -1), (0, 1)):
        for dz in (-1, 0, 1):
            for dy in (-1, 0, 1):
                t = tap(dz, dx, dy)
                wide[side, 3 * (dz + 1) + dy + 1] = jnp.broadcast_to(
                    by_channel[:, t : t + 1], (C, lanes)
                )

    half = C // 2
    pick_row = iota((2 * half, half * SUB), 0)
    pick_col = iota((2 * half, half * SUB), 1)
    same = (pick_row % half) == (pick_col // SUB)

    def picks(first, b):
        hit = same & ((pick_col % SUB) + SUB * b == first + pick_row // half)
        return jnp.where(hit, 1.0, 0.0).astype(BF16)

    pick_rim = [picks(0, 0), jnp.concatenate([picks(width - 2, b) for b in range(blocks)], axis=1)]
    lane = iota((C, lanes), 1)
    ends_row, ends_lane = iota((16, lanes), 0), iota((16, lanes), 1)
    ends = [
        jnp.where(
            (ends_row < 2) & (ends_lane == ends_row + e * (lanes - 2)), 1.0, 0.0
        ).astype(BF16)
        for e in range(2)
    ]
    for side in (1, 0):
        for z in range(ZOUT):
            for p in planes[z]:
                if side == 1:
                    for b in range(blocks):
                        loads[p, b].wait()
                for h in range(2):
                    part = [
                        field[p, b, pl.ds(h * half, half)].reshape(half * SUB, lanes)
                        for b in range(blocks if side == 1 else 1)
                    ]
                    found = dot(
                        pick_rim[side], jnp.concatenate(part, axis=0) if side == 1 else part[0]
                    )
                    for r in range(2):
                        rim[side, p, r, pl.ds(h * half, half), :] = found[r * half : (r + 1) * half]
            for r in range(2):
                sums = [None, None, None]
                for dz in (-1, 0, 1):
                    cells = rim[side, z + 2 + 2 * dz, r]
                    for dy in (-1, 0, 1):
                        term = wide[side, 3 * (dz + 1) + dy + 1] * cells
                        sums[dy + 1] = term if sums[dy + 1] is None else sums[dy + 1] + term
                total = sums[1]
                total = total + jnp.where(lane < lanes - 2, pltpu.roll(sums[2], lanes - 2, 1), 0.0)
                total = total + jnp.where(lane >= 2, pltpu.roll(sums[0], 2, 1), 0.0)
                row_send[side, z, pl.ds(r * C, C), :] = total.astype(BF16)
                at = pl.ds(z * 2 * C + r * C, C)
                rim_edge[side, 0, at, :] = sums[2].astype(BF16)
                rim_edge[side, 1, at, :] = sums[0].astype(BF16)
            if side == 1 and z == 0:
                pl.semaphore_wait(barrier, jnp.where(first, ny - 1 + 3, ny - 1 + 6))
            if side == 1:
                rows_out[ZOUT + z].start()
            if side == 1 and z == 0:
                @pl.when(lax.rem(gx, span) == span - 1)
                def _():
                    for y in (gy,) + lefts:
                        pl.semaphore_signal(here, inc=1, device_id=(sides[1], y), device_id_type=MESH)

        for e in range(2):
            corn_send[side, e] = dot(ends[e], rim_edge[side, e], NT)[:2]

    for copy in corners_out[2:]:
        copy.start()

    @pl.when(jnp.logical_not(first))
    def _():
        for copy in rows_out[:ZOUT] + corners_out[:2]:
            copy.start()

    for copy in coarse_out:
        copy.start()

    spread = (iota((C, block), 0) == iota((C, block), 1) // SUB).astype(F32)
    by_lane = dot(dw_v[...], spread, NN, HIGH)
    both = jnp.where(
        ((ends_row < 2) & (ends_lane == ends_row))
        | ((ends_row >= 2) & (ends_row < 4) & (ends_lane == ends_row + lanes - 4)),
        1.0, 0.0,
    ).astype(BF16)
    in_block = iota((SUB, block), 1) % SUB
    for p in range(ZIN):
        for b in range(blocks):
            found = dot(both, field[p, b].reshape(block, lanes), NT)[:SUB]
            edge[p, b] = jnp.where(in_block + SUB * b < width, found, 0.0)
    first_two = iota((SUB, block), 0) < 2
    weight = {}
    for dz in (-1, 0, 1):
        for dx in (-1, 0, 1):
            high, low = tap(dz, dx, 1), tap(dz, dx, -1)
            weight[dz, dx] = jnp.where(
                first_two,
                jnp.broadcast_to(by_lane[high : high + 1], (SUB, block)),
                jnp.broadcast_to(by_lane[low : low + 1], (SUB, block)),
            )
    col_send[...] = jnp.zeros_like(col_send)
    for z in range(ZOUT):
        sums = {}
        for dx in (-1, 0, 1):
            for b in range(blocks):
                total = weight[-1, dx] * edge[z, b]
                total = total + weight[0, dx] * edge[z + 2, b]
                sums[dx, b] = total + weight[1, dx] * edge[z + 4, b]
        for b in range(blocks):
            total = sums[0, b]
            total = total + jnp.where(in_block < 6, pltpu.roll(sums[1, b], block - 2, 1), 0.0)
            total = total + jnp.where(in_block >= 2, pltpu.roll(sums[-1, b], 2, 1), 0.0)
            if b + 1 < blocks:
                total = total + jnp.where(in_block >= 6, pltpu.roll(sums[1, b + 1], 6, 1), 0.0)
            if b > 0:
                total = total + jnp.where(
                    in_block < 2, pltpu.roll(sums[-1, b - 1], block - 6, 1), 0.0
                )
            at = pl.ds(2 * (z * blocks + b), 2)
            col_send[0, at, :] = total[0:2]
            col_send[1, at, :] = total[2:4]
    for copy in cols_out:
        copy.start()

    for copy in fetch[4:]:
        copy.wait()
    stage[...] = jnp.zeros_like(stage)
    slot = iota((2, SUB, lanes), 1)
    line = iota((blocks * SUB, lanes), 1)

    def taps(i, carry):
        c0 = 2 * i
        for p in range(ZIN):
            for b in range(blocks):
                cells = field[p, b, pl.ds(c0, 2)].astype(F32)
                if b > 0:
                    cells = jnp.where(slot + SUB * b < width, cells, 0.0)
                for h in range(2):
                    stage[h, p, pl.ds(SUB * (b + 1), SUB), :] = cells[h]
        for z in range(ZOUT):
            totals = []
            for h in range(2):
                sums = [None, None, None]
                for dz in (-1, 0, 1):
                    for dx in (-1, 0, 1):
                        cells = stage[h, z + 2 + 2 * dz, pl.ds(SUB + 2 * dx, SUB * blocks), :]
                        for dy in (-1, 0, 1):
                            term = dw_s[tap(dz, dx, dy), c0 + h] * cells
                            sums[dy + 1] = term if sums[dy + 1] is None else sums[dy + 1] + term
                total = sums[1] + bias_s[c0 + h]
                total = total + jnp.where(line < lanes - 2, pltpu.roll(sums[2], lanes - 2, 1), 0.0)
                total = total + jnp.where(line >= 2, pltpu.roll(sums[0], 2, 1), 0.0)
                totals.append(total)
            for b in range(blocks):
                pair = jnp.stack([total[SUB * b : SUB * (b + 1)] for total in totals])
                local[b, pl.ds(c0, 2), :, pl.ds(z * lanes, lanes)] = pair.astype(BF16)
        return carry

    lax.fori_loop(0, C // 2, taps, 0)

    tall = (iota((block, C), 0) // SUB == iota((block, C), 1)).astype(BF16)
    wide_mix = dot(tall, pw_v[...]).astype(BF16)
    flat = (iota((C, block), 1) // SUB == iota((C, block), 0)).astype(BF16)
    keep = iota((block, block), 0) % SUB == iota((block, block), 1) % SUB
    full = jnp.where(keep, dot(wide_mix, flat), 0.0).astype(BF16)
    for b in range(blocks):
        mixed[b] = dot(full, local[b].reshape(block, ZOUT * lanes)).reshape(C, SUB, ZOUT * lanes)
    four = (iota((C, 4 * C), 1) % C == iota((C, 4 * C), 0)).astype(BF16)
    arriving = dot(wide_mix, four)
    put_row, put_col = iota((block, 4 * C), 0), iota((block, 4 * C), 1)
    target = jnp.where(put_col < 2 * C, put_col // C, width - 4 + put_col // C)
    for b in range(blocks):
        hit = (put_row % SUB) + SUB * b == target
        near_w[b] = jnp.where(hit, arriving, 0.0).astype(BF16)

    for copy in coarse_out:
        copy.wait_recv()
    start = jnp.int32(0)
    for d in range(nx):
        start = start + jnp.where(d < gx, widths[d], 0)
    ncols = coarse_all.shape[2]
    held = coarse_all[...].reshape(ny * SUB, ncols)
    column = (
        iota((ncols, lanes), 0) == gy * (lanes // CF) + iota((ncols, lanes), 1) // CF
    ).astype(F32)
    count = blocks * SUB
    up_row, up_col = iota((3 * count, ny * SUB), 0), iota((3 * count, ny * SUB), 1)
    cell = start + up_row % count
    cell = jnp.where(cell >= XW * nx, cell - XW * nx, cell) // CF
    hit = (up_col // SUB == cell // rows) & (up_col % SUB == (up_row // count) * rows + cell % rows)
    along_y = dot(held, column, NN, HIGH)
    up = dot(jnp.where(hit, 1.0, 0.0), along_y, NN, HIGH)
    ups = [
        [up[k * count + b * SUB : k * count + (b + 1) * SUB] for b in range(blocks)] for k in range(3)
    ]

    def ready(i, carry):
        for b in range(blocks):
            lifted = []
            for h in range(2):
                c = 2 * i + h
                total = lift_s[0, c] * ups[0][b] + lift_s[1, c] * ups[1][b]
                lifted.append(total + lift_s[2, c] * ups[2][b])
            for z in range(ZOUT):
                at = pl.ds(z * lanes, lanes)
                cells = field[ZOUT + z, b, pl.ds(2 * i, 2)].astype(F32)
                for h in range(2):
                    c = 2 * i + h
                    base[b, c, :, at] = cells[h] + lifted[h]
                    mixed[b, c, :, at] = mixed[b, c, :, at] + pwb_s[c]
        return carry

    lax.fori_loop(0, C // 2, ready, 0)

    back_row, back_lane = iota((4, lanes), 0), iota((4, lanes), 1)
    back = jnp.where(
        back_lane == jnp.where(back_row < 2, back_row, back_row + lanes - 4), 1.0, 0.0
    ).astype(BF16)
    ends_k, ends_l = iota((32, ZOUT * lanes), 0), iota((32, ZOUT * lanes), 1)
    spot = ends_l % lanes - (ends_k // 16) * (lanes - 2)

    @pl.when(first)
    def _():
        pl.semaphore_wait(here, 3)
        for copy in rows_out[:ZOUT] + corners_out[:2]:
            copy.start()

    for copy in corners_out + cols_out:
        copy.wait_recv()
    cols = jnp.concatenate([col_recv[0], col_recv[1]], axis=0).astype(BF16)
    mixed_cols = dot(full, cols, NT).astype(BF16)
    corners = [
        dot(
            jnp.concatenate([corn_recv[side, 0], corn_recv[side, 1]], axis=0).astype(BF16), back, TN
        )
        for side in range(2)
    ]
    for copy in rows_out:
        copy.wait_recv()
    arrived = []
    for side in range(2):
        parts = [
            row_recv[side, z].astype(F32)
            + corners[side][2 * C * z : 2 * C * (z + 1)]
            for z in range(ZOUT)
        ]
        arrived.append(jnp.concatenate(parts, axis=1).astype(BF16))
    stores = []
    for b in range(blocks):
        at_lane = (ends_k % 16) // 2 == (ends_l // lanes) * blocks + b
        pick = jnp.where(at_lane & (spot == ends_k % 2), 1.0, 0.0).astype(BF16)
        right = jnp.concatenate(arrived + [pick], axis=0)
        v = dot(jnp.concatenate([near_w[b], mixed_cols], axis=1), right)
        v = v + mixed[b].reshape(block, ZOUT * lanes)
        v = base[b].reshape(block, ZOUT * lanes) + jnp.maximum(v, 0.2 * v)
        for z in range(ZOUT):
            tile = v[:, z * lanes : (z + 1) * lanes].reshape(C, SUB, lanes)
            if b > 0:
                tile = jnp.where(iota((1, SUB, lanes), 1) + SUB * b < width, tile, 0.0)
            result[z, b] = tile.astype(BF16)
            stores.append(
                pltpu.make_async_copy(
                    result.at[z, b], out.at[z, :, pl.ds(SUB * b, SUB), :], out_sem.at[z, b]
                )
            )
            stores[-1].start()

    for copy in rows_out + corners_out + cols_out + coarse_out:
        copy.wait_send()
    for store in stores:
        store.wait()


def shards(feature, widths, dw_weight, dw_bias, pw_weight, pw_bias, lift_weight, coarse):
    nx, ny = lax.axis_size("gx"), lax.axis_size("gy")
    slots, lanes = feature.shape[2], feature.shape[3]
    blocks = slots // SUB
    block = C * SUB
    both = ZOUT * lanes
    ncols = coarse.shape[2]
    lift = lift_weight.T
    dma = pltpu.SemaphoreType.DMA
    vmem, smem = pltpu.VMEM, pltpu.SMEM
    return pl.pallas_call(
        functools.partial(block_kernel, nx, ny),
        out_shape=jax.ShapeDtypeStruct((ZOUT, C, slots, lanes), BF16),
        in_specs=[pl.BlockSpec(memory_space=pltpu.HBM)] * 8,
        out_specs=pl.BlockSpec(memory_space=pl.ANY),
        scratch_shapes=[
            smem(widths.shape, jnp.int32),
            smem(dw_weight.shape, F32),
            smem(dw_bias.shape, F32),
            smem(pw_bias.shape, F32),
            smem(lift.shape, F32),
            vmem(dw_weight.shape, F32),
            vmem(pw_weight.shape, BF16),
            vmem(coarse.shape, F32),
            vmem((ZIN, blocks, C, SUB, lanes), BF16),
            vmem((blocks, C, SUB, both), BF16),
            vmem((blocks, C, SUB, both), F32),
            vmem((blocks, C, SUB, both), F32),
            vmem((ZOUT, blocks, C, SUB, lanes), BF16),
            vmem((2, ZIN, 2, C, lanes), F32),
            vmem((2, 9, C, lanes), F32),
            vmem((blocks, block, 4 * C), BF16),
            vmem((2, ZIN, (blocks + 2) * SUB, lanes), F32),
            vmem((2, 2, ZOUT * 2 * C, lanes), BF16),
            vmem((ZIN, blocks, SUB, block), F32),
            vmem((2, ZOUT, 2 * C, lanes), BF16),
            vmem((2, ZOUT, 2 * C, lanes), BF16),
            vmem((2, 2, 2, ZOUT * 2 * C), F32),
            vmem((2, 2, 2, ZOUT * 2 * C), F32),
            vmem((2, 16, block), F32),
            vmem((2, 16, block), F32),
            vmem((SUB, ncols), F32),
            vmem((ny, SUB, ncols), F32),
            dma((8,)),
            dma((ZIN, blocks)),
            dma((2, ZOUT)), dma((2, ZOUT)), dma((2, 2)), dma((2, 2)), dma((2,)), dma((2,)),
            dma((ny - 1,)), dma((ny - 1,)),
            dma((ZOUT, blocks)),
            pltpu.SemaphoreType.REGULAR,
        ],
        compiler_params=pltpu.CompilerParams(
            collective_id=0, has_side_effects=True, vmem_limit_bytes=VMEM_LIMIT
        ),
        name="block",
    )(
        *[
            pltpu.with_memory_space_constraint(a, pltpu.HBM)
            for a in (widths, dw_weight, dw_bias, pw_weight, pw_bias, lift, coarse, feature)
        ]
    )


def solution(mesh):
    placed = (P(None, None, "gx", "gy"), P(), P(), P(), P(), P(), P(), P(None, "gy", None))
    return jax.shard_map(
        shards, mesh=mesh, in_specs=placed, out_specs=P(None, None, "gx", "gy"), check_vma=False
    )
```

```python
import functools

import jax
import jax.numpy as jnp
from jax import lax
from jax.experimental import pallas as pl
from jax.experimental.pallas import tpu as pltpu
from jax.sharding import PartitionSpec as P

MESH = pl.DeviceIdType.MESH
XW = 16
ZIN = 6
ZOUT = 2
C = 64
CF = 16
VMEM_LIMIT = 50000 * 1024
SUB = 8
F32 = jnp.float32
BF16 = jnp.bfloat16
HIGH = lax.Precision.HIGHEST
NN = (((1,), (0,)), ((), ()))
NT = (((1,), (1,)), ((), ()))
TN = (((0,), (0,)), ((), ()))


def iota(shape, dim):
    return lax.broadcasted_iota(jnp.int32, shape, dim)


def dot(a, b, dims=NN, precision=None):
    return lax.dot_general(a, b, dims, precision=precision, preferred_element_type=F32)


def tap(dz, dx, dy):
    return 9 * (dz + 1) + 3 * (dx + 1) + (dy + 1)


def block_kernel(
    nx, ny,
    widths_h, dw_h, dwb_h, pw_h, pwb_h, lift_h, coarse_h, feat,
    out,
    widths, dw_s, bias_s, pwb_s, lift_s, dw_v, pw_v, coarse,
    field, local, mixed, base, result, rim, wide, near_w, stage, rim_edge, edge,
    row_send, row_recv, corn_send, corn_recv, col_send, col_recv, own, coarse_all,
    arg_sem, field_sem, row_ssem, row_rsem, corn_ssem, corn_rsem, col_ssem, col_rsem,
    co_ssem, co_rsem, out_sem, here,
):
    lanes = feat.shape[3]
    blocks = feat.shape[2] // SUB
    block = C * SUB
    gx, gy = lax.axis_index("gx"), lax.axis_index("gy")
    sides = (lax.rem(gx + nx - 1, nx), lax.rem(gx + 1, nx))

    def along(k):
        return lax.rem(gy + k, ny)

    lefts = (along(ny - 1), along(1))

    given = (
        (widths_h, widths), (dw_h, dw_v), (dw_h, dw_s), (coarse_h, coarse), (dwb_h, bias_s),
        (pwb_h, pwb_s), (lift_h, lift_s), (pw_h, pw_v),
    )
    fetch = [pltpu.make_async_copy(a, b, arg_sem.at[i]) for i, (a, b) in enumerate(given)]
    for copy in fetch[:4]:
        copy.start()
    planes = [[z + 2 * k for k in range(3)] for z in range(ZOUT)]
    loads = {}
    for p in planes[0] + planes[1]:
        for b in range(blocks):
            loads[p, b] = pltpu.make_async_copy(
                feat.at[p, :, pl.ds(SUB * b, SUB), :], field.at[p, b], field_sem.at[p, b]
            )
            loads[p, b].start()

    barrier = pltpu.get_barrier_semaphore()
    span = nx // 2 if nx % 2 == 0 else nx
    first = lax.rem(gx, span) == 0
    for y in (gy,) + lefts:
        pl.semaphore_signal(barrier, inc=1, device_id=(sides[0], y), device_id_type=MESH)

    @pl.when(lax.rem(gx, span) != span - 1)
    def _():
        for y in (gy,) + lefts:
            pl.semaphore_signal(barrier, inc=1, device_id=(sides[1], y), device_id_type=MESH)

    for k in range(1, ny):
        pl.semaphore_signal(barrier, inc=1, device_id=(gx, along(k)), device_id_type=MESH)
    for copy in fetch[4:]:
        copy.start()
    for copy in fetch[:4]:
        copy.wait()
    width = widths[gx]

    def send(src, dst, ssem, rsem, to):
        return pltpu.make_async_remote_copy(
            src_ref=src, dst_ref=dst, send_sem=ssem, recv_sem=rsem, device_id=to,
            device_id_type=MESH,
        )

    rows_out = [
        send(
            row_send.at[s, z], row_recv.at[1 - s, z], row_ssem.at[s, z], row_rsem.at[1 - s, z],
            (sides[s], gy),
        )
        for s in range(2) for z in range(ZOUT)
    ]
    corners_out = [
        send(
            corn_send.at[s, e], corn_recv.at[1 - s, 1 - e], corn_ssem.at[s, e],
            corn_rsem.at[1 - s, 1 - e], (sides[s], lefts[e]),
        )
        for s in range(2) for e in range(2)
    ]
    cols_out = [
        send(col_send.at[e], col_recv.at[1 - e], col_ssem.at[e], col_rsem.at[1 - e], (gx, lefts[e]))
        for e in range(2)
    ]
    coarse_out = [
        send(own, coarse_all.at[gy], co_ssem.at[k - 1], co_rsem.at[k - 1], (gx, along(k)))
        for k in range(1, ny)
    ]
    rows = coarse.shape[1]
    own[...] = jnp.zeros_like(own)
    for k in range(3):
        own[pl.ds(k * rows, rows), :] = coarse[k]
    coarse_all[gy] = own[...]

    eye = (iota((C, C), 0) == iota((C, C), 1)).astype(F32)
    by_channel = dot(eye, dw_v[...], NT, HIGH)

    def widen(side, dx):
        for dz in (-1, 0, 1):
            for dy in (-1, 0, 1):
                t = tap(dz, dx, dy)
                wide[side, 3 * (dz + 1) + dy + 1] = jnp.broadcast_to(
                    by_channel[:, t : t + 1], (C, lanes)
                )

    widen(1, -1)

    half = C // 2
    pick_row = iota((2 * half, half * SUB), 0)
    pick_col = iota((2 * half, half * SUB), 1)
    same = (pick_row % half) == (pick_col // SUB)

    def picks(first, b):
        hit = same & ((pick_col % SUB) + SUB * b == first + pick_row // half)
        return jnp.where(hit, 1.0, 0.0).astype(BF16)

    pick_rim = [picks(0, 0), jnp.concatenate([picks(width - 2, b) for b in range(blocks)], axis=1)]
    lane = iota((C, lanes), 1)
    ends_row, ends_lane = iota((16, lanes), 0), iota((16, lanes), 1)
    ends = [
        jnp.where(
            (ends_row < 2) & (ends_lane == ends_row + e * (lanes - 2)), 1.0, 0.0
        ).astype(BF16)
        for e in range(2)
    ]
    for side in (1, 0):
        if side == 0:
            widen(0, 1)
        for z in range(ZOUT):
            for p in planes[z]:
                if side == 1:
                    for b in range(blocks):
                        loads[p, b].wait()
                for h in range(2):
                    part = [
                        field[p, b, pl.ds(h * half, half)].reshape(half * SUB, lanes)
                        for b in range(blocks if side == 1 else 1)
                    ]
                    found = dot(
                        pick_rim[side], jnp.concatenate(part, axis=0) if side == 1 else part[0]
                    )
                    for r in range(2):
                        rim[side, p, r, pl.ds(h * half, half), :] = found[r * half : (r + 1) * half]
            for r in range(2):
                sums = [None, None, None]
                for dz in (-1, 0, 1):
                    cells = rim[side, z + 2 + 2 * dz, r]
                    for dy in (-1, 0, 1):
                        term = wide[side, 3 * (dz + 1) + dy + 1] * cells
                        sums[dy + 1] = term if sums[dy + 1] is None else sums[dy + 1] + term
                total = sums[1]
                total = total + jnp.where(lane < lanes - 2, pltpu.roll(sums[2], lanes - 2, 1), 0.0)
                total = total + jnp.where(lane >= 2, pltpu.roll(sums[0], 2, 1), 0.0)
                row_send[side, z, pl.ds(r * C, C), :] = total.astype(BF16)
                at = pl.ds(z * 2 * C + r * C, C)
                rim_edge[side, 0, at, :] = sums[2].astype(BF16)
                rim_edge[side, 1, at, :] = sums[0].astype(BF16)
            if side == 1 and z == 0:
                pl.semaphore_wait(barrier, jnp.where(first, ny - 1 + 3, ny - 1 + 6))
            if side == 1:
                rows_out[ZOUT + z].start()
            if side == 1 and z == 0:
                @pl.when(lax.rem(gx, span) == span - 1)
                def _():
                    for y in (gy,) + lefts:
                        pl.semaphore_signal(here, inc=1, device_id=(sides[1], y), device_id_type=MESH)

        for e in range(2):
            corn_send[side, e] = dot(ends[e], rim_edge[side, e], NT)[:2]

    for copy in corners_out[2:]:
        copy.start()

    @pl.when(jnp.logical_not(first))
    def _():
        for copy in rows_out[:ZOUT] + corners_out[:2]:
            copy.start()

    for copy in coarse_out:
        copy.start()

    spread = (iota((C, block), 0) == iota((C, block), 1) // SUB).astype(F32)
    by_lane = dot(dw_v[...], spread, NN, HIGH)
    both = jnp.where(
        ((ends_row < 2) & (ends_lane == ends_row))
        | ((ends_row >= 2) & (ends_row < 4) & (ends_lane == ends_row + lanes - 4)),
        1.0, 0.0,
    ).astype(BF16)
    in_block = iota((SUB, block), 1) % SUB
    for p in range(ZIN):
        for b in range(blocks):
            found = dot(both, field[p, b].reshape(block, lanes), NT)[:SUB]
            edge[p, b] = jnp.where(in_block + SUB * b < width, found, 0.0)
    first_two = iota((SUB, block), 0) < 2
    weight = {}
    for dz in (-1, 0, 1):
        for dx in (-1, 0, 1):
            high, low = tap(dz, dx, 1), tap(dz, dx, -1)
            weight[dz, dx] = jnp.where(
                first_two,
                jnp.broadcast_to(by_lane[high : high + 1], (SUB, block)),
                jnp.broadcast_to(by_lane[low : low + 1], (SUB, block)),
            )
    col_send[...] = jnp.zeros_like(col_send)
    for z in range(ZOUT):
        sums = {}
        for dx in (-1, 0, 1):
            for b in range(blocks):
                total = weight[-1, dx] * edge[z, b]
                total = total + weight[0, dx] * edge[z + 2, b]
                sums[dx, b] = total + weight[1, dx] * edge[z + 4, b]
        for b in range(blocks):
            total = sums[0, b]
            total = total + jnp.where(in_block < 6, pltpu.roll(sums[1, b], block - 2, 1), 0.0)
            total = total + jnp.where(in_block >= 2, pltpu.roll(sums[-1, b], 2, 1), 0.0)
            if b + 1 < blocks:
                total = total + jnp.where(in_block >= 6, pltpu.roll(sums[1, b + 1], 6, 1), 0.0)
            if b > 0:
                total = total + jnp.where(
                    in_block < 2, pltpu.roll(sums[-1, b - 1], block - 6, 1), 0.0
                )
            at = pl.ds(2 * (z * blocks + b), 2)
            col_send[0, at, :] = total[0:2]
            col_send[1, at, :] = total[2:4]
    for copy in cols_out:
        copy.start()

    for copy in fetch[4:]:
        copy.wait()
    stage[...] = jnp.zeros_like(stage)
    slot = iota((2, SUB, lanes), 1)
    line = iota((blocks * SUB, lanes), 1)

    def taps(i, carry):
        c0 = 2 * i
        for p in range(ZIN):
            for b in range(blocks):
                cells = field[p, b, pl.ds(c0, 2)].astype(F32)
                if b > 0:
                    cells = jnp.where(slot + SUB * b < width, cells, 0.0)
                for h in range(2):
                    stage[h, p, pl.ds(SUB * (b + 1), SUB), :] = cells[h]
        for z in range(ZOUT):
            totals = []
            for h in range(2):
                sums = [None, None, None]
                for dz in (-1, 0, 1):
                    for dx in (-1, 0, 1):
                        cells = stage[h, z + 2 + 2 * dz, pl.ds(SUB + 2 * dx, SUB * blocks), :]
                        for dy in (-1, 0, 1):
                            term = dw_s[tap(dz, dx, dy), c0 + h] * cells
                            sums[dy + 1] = term if sums[dy + 1] is None else sums[dy + 1] + term
                total = sums[1] + bias_s[c0 + h]
                total = total + jnp.where(line < lanes - 2, pltpu.roll(sums[2], lanes - 2, 1), 0.0)
                total = total + jnp.where(line >= 2, pltpu.roll(sums[0], 2, 1), 0.0)
                totals.append(total)
            for b in range(blocks):
                pair = jnp.stack([total[SUB * b : SUB * (b + 1)] for total in totals])
                local[b, pl.ds(c0, 2), :, pl.ds(z * lanes, lanes)] = pair.astype(BF16)
        return carry

    lax.fori_loop(0, C // 2, taps, 0)

    tall = (iota((block, C), 0) // SUB == iota((block, C), 1)).astype(BF16)
    wide_mix = dot(tall, pw_v[...]).astype(BF16)
    flat = (iota((C, block), 1) // SUB == iota((C, block), 0)).astype(BF16)
    keep = iota((block, block), 0) % SUB == iota((block, block), 1) % SUB
    full = jnp.where(keep, dot(wide_mix, flat), 0.0).astype(BF16)
    for b in range(blocks):
        mixed[b] = dot(full, local[b].reshape(block, ZOUT * lanes)).reshape(C, SUB, ZOUT * lanes)
    four = (iota((C, 4 * C), 1) % C == iota((C, 4 * C), 0)).astype(BF16)
    arriving = dot(wide_mix, four)
    put_row, put_col = iota((block, 4 * C), 0), iota((block, 4 * C), 1)
    target = jnp.where(put_col < 2 * C, put_col // C, width - 4 + put_col // C)
    for b in range(blocks):
        hit = (put_row % SUB) + SUB * b == target
        near_w[b] = jnp.where(hit, arriving, 0.0).astype(BF16)

    for copy in coarse_out:
        copy.wait_recv()
    start = jnp.int32(0)
    for d in range(nx):
        start = start + jnp.where(d < gx, widths[d], 0)
    ncols = coarse_all.shape[2]
    held = coarse_all[...].reshape(ny * SUB, ncols)
    column = (
        iota((ncols, lanes), 0) == gy * (lanes // CF) + iota((ncols, lanes), 1) // CF
    ).astype(F32)
    count = blocks * SUB
    up_row, up_col = iota((3 * count, ny * SUB), 0), iota((3 * count, ny * SUB), 1)
    cell = start + up_row % count
    cell = jnp.where(cell >= XW * nx, cell - XW * nx, cell) // CF
    hit = (up_col // SUB == cell // rows) & (up_col % SUB == (up_row // count) * rows + cell % rows)
    along_y = dot(held, column, NN, HIGH)
    up = dot(jnp.where(hit, 1.0, 0.0), along_y, NN, HIGH)
    ups = [
        [up[k * count + b * SUB : k * count + (b + 1) * SUB] for b in range(blocks)] for k in range(3)
    ]

    def ready(i, carry):
        for b in range(blocks):
            lifted = []
            for h in range(2):
                c = 2 * i + h
                total = lift_s[0, c] * ups[0][b] + lift_s[1, c] * ups[1][b]
                lifted.append(total + lift_s[2, c] * ups[2][b])
            for z in range(ZOUT):
                at = pl.ds(z * lanes, lanes)
                cells = field[ZOUT + z, b, pl.ds(2 * i, 2)].astype(F32)
                for h in range(2):
                    c = 2 * i + h
                    base[b, c, :, at] = cells[h] + lifted[h]
                    mixed[b, c, :, at] = mixed[b, c, :, at] + pwb_s[c]
        return carry

    lax.fori_loop(0, C // 2, ready, 0)

    back_row, back_lane = iota((4, lanes), 0), iota((4, lanes), 1)
    back = jnp.where(
        back_lane == jnp.where(back_row < 2, back_row, back_row + lanes - 4), 1.0, 0.0
    ).astype(BF16)
    ends_k, ends_l = iota((32, ZOUT * lanes), 0), iota((32, ZOUT * lanes), 1)
    spot = ends_l % lanes - (ends_k // 16) * (lanes - 2)

    @pl.when(first)
    def _():
        pl.semaphore_wait(here, 3)
        for copy in rows_out[:ZOUT] + corners_out[:2]:
            copy.start()

    for copy in corners_out + cols_out:
        copy.wait_recv()
    cols = jnp.concatenate([col_recv[0], col_recv[1]], axis=0).astype(BF16)
    mixed_cols = dot(full, cols, NT).astype(BF16)
    corners = [
        dot(
            jnp.concatenate([corn_recv[side, 0], corn_recv[side, 1]], axis=0).astype(BF16), back, TN
        )
        for side in range(2)
    ]
    for copy in rows_out:
        copy.wait_recv()
    arrived = []
    for side in range(2):
        parts = [
            row_recv[side, z].astype(F32)
            + corners[side][2 * C * z : 2 * C * (z + 1)]
            for z in range(ZOUT)
        ]
        arrived.append(jnp.concatenate(parts, axis=1).astype(BF16))
    stores = []
    for b in range(blocks):
        at_lane = (ends_k % 16) // 2 == (ends_l // lanes) * blocks + b
        pick = jnp.where(at_lane & (spot == ends_k % 2), 1.0, 0.0).astype(BF16)
        right = jnp.concatenate(arrived + [pick], axis=0)
        v = dot(jnp.concatenate([near_w[b], mixed_cols], axis=1), right)
        v = v + mixed[b].reshape(block, ZOUT * lanes)
        v = base[b].reshape(block, ZOUT * lanes) + jnp.maximum(v, 0.2 * v)
        for z in range(ZOUT):
            tile = v[:, z * lanes : (z + 1) * lanes].reshape(C, SUB, lanes)
            if b > 0:
                tile = jnp.where(iota((1, SUB, lanes), 1) + SUB * b < width, tile, 0.0)
            result[z, b] = tile.astype(BF16)
            stores.append(
                pltpu.make_async_copy(
                    result.at[z, b], out.at[z, :, pl.ds(SUB * b, SUB), :], out_sem.at[z, b]
                )
            )
            stores[-1].start()

    for copy in rows_out + corners_out + cols_out + coarse_out:
        copy.wait_send()
    for store in stores:
        store.wait()


def shards(feature, widths, dw_weight, dw_bias, pw_weight, pw_bias, lift_weight, coarse):
    nx, ny = lax.axis_size("gx"), lax.axis_size("gy")
    slots, lanes = feature.shape[2], feature.shape[3]
    blocks = slots // SUB
    block = C * SUB
    both = ZOUT * lanes
    ncols = coarse.shape[2]
    lift = lift_weight.T
    dma = pltpu.SemaphoreType.DMA
    vmem, smem = pltpu.VMEM, pltpu.SMEM
    return pl.pallas_call(
        functools.partial(block_kernel, nx, ny),
        out_shape=jax.ShapeDtypeStruct((ZOUT, C, slots, lanes), BF16),
        in_specs=[pl.BlockSpec(memory_space=pltpu.HBM)] * 8,
        out_specs=pl.BlockSpec(memory_space=pl.ANY),
        scratch_shapes=[
            smem(widths.shape, jnp.int32),
            smem(dw_weight.shape, F32),
            smem(dw_bias.shape, F32),
            smem(pw_bias.shape, F32),
            smem(lift.shape, F32),
            vmem(dw_weight.shape, F32),
            vmem(pw_weight.shape, BF16),
            vmem(coarse.shape, F32),
            vmem((ZIN, blocks, C, SUB, lanes), BF16),
            vmem((blocks, C, SUB, both), BF16),
            vmem((blocks, C, SUB, both), F32),
            vmem((blocks, C, SUB, both), F32),
            vmem((ZOUT, blocks, C, SUB, lanes), BF16),
            vmem((2, ZIN, 2, C, lanes), F32),
            vmem((2, 9, C, lanes), F32),
            vmem((blocks, block, 4 * C), BF16),
            vmem((2, ZIN, (blocks + 2) * SUB, lanes), F32),
            vmem((2, 2, ZOUT * 2 * C, lanes), BF16),
            vmem((ZIN, blocks, SUB, block), F32),
            vmem((2, ZOUT, 2 * C, lanes), BF16),
            vmem((2, ZOUT, 2 * C, lanes), BF16),
            vmem((2, 2, 2, ZOUT * 2 * C), F32),
            vmem((2, 2, 2, ZOUT * 2 * C), F32),
            vmem((2, 16, block), F32),
            vmem((2, 16, block), F32),
            vmem((SUB, ncols), F32),
            vmem((ny, SUB, ncols), F32),
            dma((8,)),
            dma((ZIN, blocks)),
            dma((2, ZOUT)), dma((2, ZOUT)), dma((2, 2)), dma((2, 2)), dma((2,)), dma((2,)),
            dma((ny - 1,)), dma((ny - 1,)),
            dma((ZOUT, blocks)),
            pltpu.SemaphoreType.REGULAR,
        ],
        compiler_params=pltpu.CompilerParams(
            collective_id=0, has_side_effects=True, vmem_limit_bytes=VMEM_LIMIT
        ),
        name="block",
    )(
        *[
            pltpu.with_memory_space_constraint(a, pltpu.HBM)
            for a in (widths, dw_weight, dw_bias, pw_weight, pw_bias, lift, coarse, feature)
        ]
    )


def solution(mesh):
    placed = (P(None, None, "gx", "gy"), P(), P(), P(), P(), P(), P(), P(None, "gy", None))
    return jax.shard_map(
        shards, mesh=mesh, in_specs=placed, out_specs=P(None, None, "gx", "gy"), check_vma=False
    )
```
